32 devices in a mesh: grp: 4 (over y, core), ch: 8 (over z, x).
Axes of the slice: x: 2, y: 2, z: 4, core: 2. Of those that a mesh axis runs over, the one named last changes fastest.
Arguments:
- strain: bfloat16 [8, 1024, 4096], P('grp', 'ch'), may hold values from -6 to 6
- valid_mask: int32 [8, 1024], P('grp', 'ch'), may hold values 0 or 1
- pair_list: int32 [8, 6, 2], P('ch'), may hold values from 0 to 7, as said below
- owner_group: int32 [8, 6], P('ch'), may hold values from 0 to 3, as said below
Outputs:
- stacks: float32 [4, 8, 2, 128, 4096], P('grp', 'ch')
The draws below stay inside these ranges and needn't reach their ends.
Inputs may be any that keep to these rules, and one draw needn't show every extreme that they name: `pair_list`: entries are channel block numbers; each ordered pair of blocks appears at most once over all columns. `owner_group`: in each column no group owns more than 2 entries, and some group owns exactly 2.
All inputs are finite; a program needn't handle non-finite values. No bound on the sum of `valid_mask` on one device may be relied on, other than what follows from the above.
Results may differ from the reference program's by a relative error of at most 0.0042.
Values may be sent and summed in bfloat16 or wider, within the bound.
A program may use at most 192 MiB of HBM per device.

```python
import math
import jax
import jax.numpy as jnp
from jax import lax

NFFT = 4096
NB = 1024
SUB = 64
BLK = 128
CAP = 2
GROUPS = 4
COLUMNS = 8
CHANNELS = 1024
WINDOWS = 8
LIST = 6


def draw_pair_list(key, part):
    blocks = CHANNELS // BLK
    pair_codes = jax.random.permutation(key, blocks * blocks)[:COLUMNS * LIST]
    first_block = pair_codes // blocks
    second_block = pair_codes % blocks
    return jnp.stack([first_block, second_block], axis=-1).reshape(COLUMNS, LIST, 2).astype(jnp.int32)


def owner_column(column_key):
    key_slots, key_order = jax.random.split(column_key)
    slot_perm = jax.random.permutation(key_slots, GROUPS * CAP)
    slot_groups = slot_perm // CAP
    head_group = slot_groups[0]
    ordering = jnp.argsort(jnp.where(slot_groups == head_group, 0, 1), stable=True)
    chosen = slot_groups[ordering][:LIST]
    return chosen[jax.random.permutation(key_order, LIST)]


def draw_owner_group(key, part):
    column_keys = jax.random.split(jax.random.fold_in(key, 7), COLUMNS)
    return jax.vmap(owner_column)(column_keys).astype(jnp.int32)


def place_ends(entries, stream_key, low, high):
    spot = [jax.random.randint(jax.random.fold_in(stream_key, axis), (), 0, length) for axis, length in enumerate(entries.shape)]
    longest = entries.shape.index(max(entries.shape))
    next_to = spot[:longest] + [(spot[longest] + 1) % entries.shape[longest]] + spot[longest + 1:]
    return entries.at[tuple(spot)].set(low).at[tuple(next_to)].set(high)


def block_scale(own_key, dims, pieces, low, largest):
    factor_of = 1.0
    for dim, shards_of in pieces:
        steps = jax.random.uniform(jax.random.fold_in(jax.random.fold_in(own_key, 6), dim), (shards_of,), jnp.float32, low / len(pieces), largest / len(pieces))
        factor_of = factor_of * jnp.repeat(jnp.exp(steps), dims[dim] // shards_of).reshape((-1,) + (1,) * (len(dims) - 1 - dim))
    return factor_of


def centred(key, shape, deviation, most, cuts=(), held_as=jnp.bfloat16):
    level = block_scale(key, shape, cuts, -0.22, 0.18) if cuts else 1.0
    drawn = jax.random.normal(key, shape, jnp.float32) * deviation * level
    return jnp.minimum(jnp.maximum(drawn, -most), most).astype(held_as)


def setup_inputs(seed: int = 0) -> dict:
    key_of = jax.random.split(jax.random.key(seed), 5)
    strain = centred(key_of[0], (WINDOWS, CHANNELS, NFFT), 1.0, 6.0, ((0, 4), (1, 8)))
    valid_mask = place_ends((jax.random.randint(key_of[1], (WINDOWS, CHANNELS), 0, 4) < 3).astype(jnp.int32), jax.random.fold_in(key_of[1], 1), 0, 1)
    pair_list = draw_pair_list(jax.random.fold_in(key_of[4], 71), 0)
    owner_group = draw_owner_group(jax.random.fold_in(key_of[4], 71), 0)
    return dict(strain=strain, valid_mask=valid_mask, pair_list=pair_list, owner_group=owner_group)


def forward_table(length, bins):
    samples = jnp.arange(length, dtype=jnp.int32)
    frequency = jnp.arange(1, bins + 1, dtype=jnp.int32)
    angles = jnp.mod(samples[:, None] * frequency[None, :], length).astype(jnp.float32) * (2.0 * math.pi / length)
    hann_taper = 0.5 - 0.5 * jnp.cos(samples.astype(jnp.float32) * (2.0 * math.pi / length))
    return jnp.concatenate([hann_taper[:, None] * jnp.cos(angles), -hann_taper[:, None] * jnp.sin(angles)], axis=1).astype(jnp.bfloat16)

def inverse_table(length, bins):
    frequency = jnp.arange(1, bins + 1, dtype=jnp.int32)
    lag_index = jnp.arange(length, dtype=jnp.int32) - length // 2
    angles = jnp.mod(frequency[:, None] * lag_index[None, :], length).astype(jnp.float32) * (2.0 * math.pi / length)
    return jnp.concatenate([jnp.cos(angles), -jnp.sin(angles)], axis=0)

def whiten_rows(spectrum, valid_mask, bins, band):
    real_part = spectrum[..., :bins]
    imag_part = spectrum[..., bins:]
    power = real_part * real_part + imag_part * imag_part
    band_power = lax.optimization_barrier(jnp.sum(power.reshape(power.shape[:-1] + (bins // band, band)), axis=-1)) / band
    norm_full = jnp.repeat(jnp.sqrt(band_power + 1e-06), band, axis=-1)
    norm_both = jnp.concatenate([norm_full, norm_full], axis=-1)
    return (spectrum / norm_both * valid_mask[..., None].astype(jnp.float32)).astype(jnp.bfloat16)

def cross_block(rows, pair_entry, block, bins):
    first_rows = lax.dynamic_slice_in_dim(rows, (pair_entry[0] * block).astype(jnp.int32), block, 1).astype(jnp.float32)
    second_rows = lax.dynamic_slice_in_dim(rows, (pair_entry[1] * block).astype(jnp.int32), block, 1).astype(jnp.float32)
    first_real = first_rows[..., :bins]
    first_imag = first_rows[..., bins:]
    second_real = second_rows[..., :bins]
    second_imag = second_rows[..., bins:]
    cross_real = lax.optimization_barrier(jnp.sum(first_real * second_real + first_imag * second_imag, axis=0))
    cross_imag = lax.optimization_barrier(jnp.sum(first_real * second_imag - first_imag * second_real, axis=0))
    return jnp.concatenate([cross_real, cross_imag], axis=-1)

def reference(strain, valid_mask, pair_list, owner_group):
    forward = forward_table(NFFT, NB).astype(jnp.float32)
    spectrum = jnp.dot(strain.reshape(-1, NFFT).astype(jnp.float32), forward, precision=lax.Precision.HIGHEST, preferred_element_type=jnp.float32)
    spectrum = spectrum.reshape(WINDOWS, CHANNELS, 2 * NB)
    white = whiten_rows(spectrum, valid_mask, NB, SUB)
    pair_codes = pair_list.reshape(-1, 2)
    cross = lax.map(lambda pair_entry: cross_block(white, pair_entry, BLK, NB), pair_codes)
    cross_flat = cross.reshape(COLUMNS, LIST, BLK * 2 * NB)
    positions = jnp.arange(LIST, dtype=jnp.int32)
    earlier = positions[None, :] < positions[:, None]
    same_owner = owner_group[:, :, None] == owner_group[:, None, :]
    slot_rank = lax.optimization_barrier(jnp.sum((same_owner & earlier[None, :, :]).astype(jnp.int32), axis=2))
    slot_ids = jnp.arange(CAP, dtype=jnp.int32)
    inverse = inverse_table(NFFT, NB)
    scale = 1.0 / math.sqrt(NB * WINDOWS)

    def one_group(group_id):
        picking = ((owner_group[:, None, :] == group_id) & (slot_rank[:, None, :] == slot_ids[None, :, None])).astype(jnp.float32)
        stack = jnp.einsum('csl,clf->csf', picking, cross_flat, precision=lax.Precision.HIGHEST)
        stacked = jnp.dot(stack.reshape(-1, 2 * NB), inverse, precision=lax.Precision.HIGHEST, preferred_element_type=jnp.float32)
        return (stacked * scale).reshape(COLUMNS, CAP, BLK, NFFT)
    return lax.map(one_group, jnp.arange(GROUPS, dtype=jnp.int32))
```

```python
import functools
import math

import jax
import jax.numpy as jnp
import numpy as np
from jax import lax
from jax.experimental import pallas as pl
from jax.experimental.pallas import tpu as pltpu
from jax.sharding import PartitionSpec as P

NFFT = 4096
NB = 1024
SUB = 64
BLK = 128
CAP = 2
LANES = 128
UNIT = 8
LAGS = 512
MESH = pl.DeviceIdType.MESH


def phases_of(devices):
    return 2 if NB // devices % (2 * UNIT) == 0 else 1


def bin_numbers(groups, columns):
    phases = phases_of(groups * columns)
    tile_bins = columns * UNIT * phases
    bins = 1 + np.arange(NB, dtype=np.int64)
    bins = bins.reshape(groups, NB // tile_bins // groups, columns, UNIT, phases)
    return bins.transpose(0, 1, 4, 2, 3)


def table_rows(bins, samples, taper):
    angles = np.mod(bins[..., None, :, None] * samples, NFFT) * (2.0 * math.pi / NFFT)
    rows = np.concatenate([np.cos(angles), -np.sin(angles)], axis=-3) * taper
    return rows.reshape(2 * bins.size, len(samples)).astype(jnp.bfloat16)


@functools.lru_cache(maxsize=None)
def forward_rows(groups, columns):
    samples = np.arange(NFFT, dtype=np.int64)
    taper = 0.5 - 0.5 * np.cos(samples * (2.0 * math.pi / NFFT))
    return table_rows(bin_numbers(groups, columns), samples, taper)


@functools.lru_cache(maxsize=None)
def inverse_rows(groups, columns):
    phases = phases_of(groups * columns)
    bins = bin_numbers(groups, columns).transpose(2, 0, 3, 1, 4)
    samples = np.arange(NFFT, dtype=np.int64) - NFFT // 2
    if phases > 1:
        samples = samples[NFFT // 2 :]
    rows = table_rows(bins, samples, np.ones(len(samples)))
    return rows.reshape(phases, 2 * NB // phases, len(samples))


def loop(low, high, body):
    def step_body(step, carry):
        body(step)
        return carry

    lax.fori_loop(low, high, step_body, 0)


def transposed(stack_ref, left_ref):
    for rank in range(CAP):
        block = stack_ref[rank].reshape(-1, BLK).astype(jnp.float32)
        left_ref[rank * BLK : (rank + 1) * BLK, :] = block.T.astype(jnp.bfloat16)


def correlate_kernel(
    groups, columns, phases, entries, windows, scale,
    pairs_hbm, owners_hbm, mask_hbm, strain_hbm, table_hbm, inverse_hbm, *rest,
):
    last_stack = rest[0]
    odd_ref = rest[1] if phases > 1 else None
    rest = list(rest[phases:])
    take = lambda count: [rest.pop(0) for _ in range(count)]
    pairs_ref, owners_ref, mask_ref, strain_ref, inverse_buf, left_buf = take(6)
    table_buf, white_buf, list_buf, lists_buf, lists_smem, slots_smem = take(6)
    rows_bufs, swap_bufs, forward_bufs = take(phases), take(phases), take(phases)
    entry_bufs = [take(columns) for _ in range(phases)]
    stack_bufs = take(phases - 1) + [last_stack]
    in_sem, inverse_sem, table_sem, own_sem, lsend_sem, lrecv_sem = take(6)
    wown_sem, wsend_sem, wrecv_sem, hsend_sem, hrecv_sem, fsend_sem, frecv_sem = take(7)
    devices = groups * columns
    my_group = lax.axis_index("grp")
    mine = lax.axis_index("ch")
    me = my_group * columns + mine
    tiles = table_buf.shape[0]
    per_group = tiles // groups
    unit_rows = 2 * UNIT

    def group_at(index):
        return lax.rem(index + my_group, groups)

    def tile_copy(index):
        place = group_at(index // per_group) * per_group + lax.rem(index, per_group)
        return pltpu.make_async_copy(
            table_hbm.at[place], table_buf.at[index], table_sem.at[index]
        )

    inputs = [
        pltpu.make_async_copy(source, target, in_sem.at[place])
        for place, (source, target) in enumerate(
            [
                (pairs_hbm, pairs_ref),
                (owners_hbm, owners_ref),
                (mask_hbm, mask_ref),
                (strain_hbm, strain_ref),
            ]
        )
    ]
    inputs[3].start()
    tile_copy(0).start()
    for copy in inputs[:3]:
        copy.start()
    barrier = pltpu.get_barrier_semaphore()

    def greet(step):
        column = lax.rem(mine + step, columns)
        for other in range(groups):
            group = group_at(other)
            if other == 0:

                @pl.when(step > 0)
                def _():
                    pl.semaphore_signal(
                        barrier, inc=1, device_id=(group, column), device_id_type=MESH
                    )

            else:
                pl.semaphore_signal(
                    barrier, inc=1, device_id=(group, column), device_id_type=MESH
                )

    loop(0, columns, greet)
    loop(1, tiles, lambda index: tile_copy(index).start())
    if phases > 1:
        inverse_copy = pltpu.make_async_copy(inverse_hbm, inverse_buf, inverse_sem.at[0])
        inverse_copy.start()
    for copy in inputs:
        copy.wait()
    lane = lax.broadcasted_iota(jnp.int32, (8, LANES), 1)
    row = jnp.zeros((8, LANES), jnp.int32)
    for entry in range(entries):
        row = jnp.where(lane == 2 * entry, pairs_ref[0, 0, entry], row)
        row = jnp.where(lane == 2 * entry + 1, pairs_ref[0, 1, entry], row)
    list_buf[...] = row

    def compute_tile(index):
        tile_copy(index).wait()
        spectrum = lax.dot_general(
            table_buf[index],
            strain_ref[...],
            (((1,), (1,)), ((), ())),
            preferred_element_type=jnp.float32,
        )
        lanes = spectrum.shape[1]
        parts = spectrum.reshape(phases, columns, 2, UNIT, lanes)
        power = parts[:, :, 0] * parts[:, :, 0] + parts[:, :, 1] * parts[:, :, 1]
        bands = phases * columns * UNIT // SUB
        power = power.reshape(phases, bands, columns // bands, UNIT, lanes)
        power = jnp.sum(jnp.sum(power, axis=2), axis=0)
        band_power = jnp.sum(power, axis=1, keepdims=True) / SUB
        usable = jnp.concatenate([mask_ref[w : w + 1, :] for w in range(windows)], axis=1)
        gain = usable.astype(jnp.float32).reshape(1, 1, lanes) / jnp.sqrt(band_power + 1e-06)
        gain = gain.reshape(1, bands, 1, 1, lanes)
        white = parts.reshape(phases, bands, columns // bands, unit_rows, lanes) * gain
        white = white.reshape(phases, columns, unit_rows, lanes).astype(jnp.bfloat16)
        at = pl.ds(pl.multiple_of(lax.rem(index, per_group) * unit_rows, unit_rows), unit_rows)
        white_buf[index // per_group, :, :, at, :] = white

    def white_copy(phase, index, column):
        return pltpu.make_async_remote_copy(
            src_ref=white_buf.at[index, phase, column],
            dst_ref=rows_bufs[phase].at[me],
            send_sem=wsend_sem.at[phase],
            recv_sem=wrecv_sem.at[phase],
            device_id=(group_at(index), column),
            device_id_type=MESH,
        )

    def white_own(phase):
        return pltpu.make_async_copy(
            white_buf.at[0, phase, mine], rows_bufs[phase].at[me], wown_sem.at[phase]
        )

    def send_white(phase, index):
        def send(step):
            white_copy(phase, index, lax.rem(mine + step, columns)).start()

        loop(1, columns, send)
        if isinstance(index, int) and index == 0:
            white_own(phase).start()
        else:
            send(0)

    def list_copy(step):
        return pltpu.make_async_remote_copy(
            src_ref=list_buf,
            dst_ref=lists_buf.at[mine],
            send_sem=lsend_sem.at[step],
            recv_sem=lrecv_sem.at[step],
            device_id=(my_group, lax.rem(mine + step, columns)),
            device_id_type=MESH,
        )

    loop(0, per_group, compute_tile)
    pl.semaphore_wait(barrier, devices - 1)
    send_white(0, 0)
    loop(1, columns, lambda step: list_copy(step).start())
    own_list = pltpu.make_async_copy(list_buf, lists_buf.at[mine], own_sem.at[0])
    own_list.start()

    def compute_and_send(index):
        loop(index * per_group, (index + 1) * per_group, compute_tile)
        send_white(0, index)

    loop(1, groups, compute_and_send)
    for phase in range(1, phases):
        send_white(phase, 0)
        loop(1, groups, lambda index, phase=phase: send_white(phase, index))

    ranks = []
    for entry in range(entries):
        rank = jnp.int32(0)
        for before in range(entry):
            rank += (owners_ref[0, before] == owners_ref[0, entry]).astype(jnp.int32)
        ranks.append(rank)
    for group in range(groups):
        for rank in range(CAP):
            chosen, used = jnp.int32(0), jnp.int32(0)
            for entry in range(entries):
                match = (owners_ref[0, entry] == group) & (ranks[entry] == rank)
                chosen = jnp.where(match, entry, chosen)
                used = jnp.where(match, 1, used)
            slots_smem[0, group * CAP + rank] = chosen
            slots_smem[1, group * CAP + rank] = used

    own_list.wait()
    loop(1, columns, lambda step: list_copy(step).wait())
    to_smem = pltpu.make_async_copy(lists_buf, lists_smem, own_sem.at[1])
    to_smem.start()
    to_smem.wait()

    def cross_column(phase, column, out_ref):
        rows_ref = rows_bufs[phase]
        for entry in range(entries):
            first = lists_smem[column, 0, 2 * entry]
            second = lists_smem[column, 0, 2 * entry + 1]
            sums = [jnp.zeros((UNIT, BLK), jnp.float32) for _ in range(2 * per_group)]
            for group in range(groups):
                a = rows_ref[group * columns + first].astype(jnp.float32)
                b = rows_ref[group * columns + second].astype(jnp.float32)
                for window in range(windows):
                    lanes = slice(window * BLK, (window + 1) * BLK)
                    for unit in range(per_group):
                        low, high = unit * unit_rows, unit * unit_rows + UNIT
                        a_real, a_imag = a[low:high, lanes], a[high : high + UNIT, lanes]
                        b_real, b_imag = b[low:high, lanes], b[high : high + UNIT, lanes]
                        sums[2 * unit] += a_real * b_real + a_imag * b_imag
                        sums[2 * unit + 1] += a_real * b_imag - a_imag * b_real
            both = jnp.concatenate(sums, axis=0) * scale
            out_ref[entry] = both.astype(jnp.bfloat16)

    def swap_copy(phase, step):
        return pltpu.make_async_remote_copy(
            src_ref=swap_bufs[phase].at[step - 1],
            dst_ref=entry_bufs[phase][step],
            send_sem=hsend_sem.at[phase],
            recv_sem=hrecv_sem.at[phase, step],
            device_id=(my_group, lax.rem(mine + step, columns)),
            device_id_type=MESH,
        )

    def arrived(ref, sem):
        return pltpu.make_async_remote_copy(
            src_ref=ref,
            dst_ref=ref,
            send_sem=sem,
            recv_sem=sem,
            device_id=(lax.rem(my_group + 1, groups), mine),
            device_id_type=MESH,
        )

    def cross_phase(phase):
        white_own(phase).wait()
        arrived(rows_bufs[phase].at[pl.ds(0, devices - 1)], wrecv_sem.at[phase]).wait_recv()

        def cross_and_send(step):
            column = lax.rem(mine + step, columns)
            cross_column(phase, column, swap_bufs[phase].at[step - 1])
            for place in range(1, columns):

                @pl.when(step == place)
                def _():
                    swap_copy(phase, place).start()

        loop(1, columns, cross_and_send)
        cross_column(phase, mine, entry_bufs[phase][0])

    def forward_copy(phase, other, source):
        return pltpu.make_async_remote_copy(
            src_ref=forward_bufs[phase].at[other - 1, source],
            dst_ref=stack_bufs[phase].at[:, my_group * columns + source],
            send_sem=fsend_sem.at[phase],
            recv_sem=frecv_sem.at[phase, my_group],
            device_id=(group_at(other), mine),
            device_id_type=MESH,
        )

    def forward_phase(phase):
        for step in range(columns):
            source = lax.rem(mine - step + columns, columns)
            if step > 0:
                swap_copy(phase, step).wait_recv()
            for other in range(groups):
                for rank in range(CAP):
                    slot = group_at(other) * CAP + rank
                    used = slots_smem[1, slot].astype(jnp.float32)
                    block = entry_bufs[phase][step][slots_smem[0, slot]].astype(jnp.float32)
                    block = (block * used).astype(jnp.bfloat16)
                    if other == 0:
                        stack_bufs[phase][rank, my_group * columns + source] = block
                    else:
                        forward_bufs[phase][other - 1, source, rank] = block
                if other > 0:
                    forward_copy(phase, other, source).start()

    def wait_stack(phase):
        def wait(other):
            group = group_at(other)
            part = stack_bufs[phase].at[:, pl.ds(group * columns, columns)]
            arrived(part, frecv_sem.at[phase, group]).wait_recv()

        loop(1, groups, wait)

    for phase in range(phases):
        cross_phase(phase)
    for phase in range(phases):
        forward_phase(phase)
        if phase < phases - 1:
            wait_stack(phase)
            inverse_copy.wait()
            transposed(stack_bufs[phase], left_buf)

            def inverse_tile(tile):
                at = pl.ds(pl.multiple_of(tile * LAGS, LAGS), LAGS)
                odd_ref[:, at] = jnp.dot(
                    left_buf[...], inverse_buf[:, at], preferred_element_type=jnp.float32
                )

            loop(0, NFFT // 2 // LAGS, inverse_tile)
    for phase in range(phases):
        arrived(rows_bufs[phase].at[pl.ds(0, devices - 1)], wsend_sem.at[phase]).wait_send()
        arrived(swap_bufs[phase], hsend_sem.at[phase]).wait_send()
        arrived(forward_bufs[phase], fsend_sem.at[phase]).wait_send()
    wait_stack(phases - 1)


def lags_kernel(stack_ref, odd_ref, inverse_ref, out_hbm, left_buf, out_buf, out_sem):
    transposed(stack_ref, left_buf)
    count = NFFT // 2 // LAGS

    def copies(tile):
        for side in range(2):
            at = pl.ds(side * (NFFT // 2) + tile * LAGS, LAGS)
            yield pltpu.make_async_copy(
                out_buf.at[:, at], out_hbm.at[:, at], out_sem.at[side, tile]
            )

    for tile in range(count):
        at = slice(tile * LAGS, (tile + 1) * LAGS)
        upper = slice(NFFT // 2 + tile * LAGS, NFFT // 2 + (tile + 1) * LAGS)
        even = jnp.dot(left_buf[...], inverse_ref[:, at], preferred_element_type=jnp.float32)
        odd = odd_ref[:, at]
        out_buf[:, at] = even - odd
        out_buf[:, upper] = even + odd
        for copy in copies(tile):
            copy.start()
    for tile in range(count):
        for copy in copies(tile):
            copy.wait()


def local(strain, valid_mask, pair_list, owner_group):
    windows, channels = valid_mask.shape
    groups = lax.axis_size("grp")
    columns = lax.axis_size("ch")
    devices = groups * columns
    entries = owner_group.shape[1]
    phases = phases_of(devices)
    rows = 2 * NB // devices // phases
    lanes = windows * channels
    tiles = NB // (columns * UNIT * phases)
    tile_rows = 2 * NB // tiles
    scale = 1.0 / math.sqrt(NB * windows * groups)

    vmem = pl.BlockSpec(memory_space=pltpu.VMEM)
    anywhere = pl.BlockSpec(memory_space=pltpu.HBM)
    dma = pltpu.SemaphoreType.DMA
    bf16 = jnp.bfloat16
    depth = devices * rows
    stack_shape = (CAP, devices, rows, BLK)
    outs = [jax.ShapeDtypeStruct(stack_shape, bf16)]
    if phases > 1:
        outs.append(jax.ShapeDtypeStruct((CAP * BLK, NFFT // 2), jnp.float32))
    inverse = inverse_rows(groups, columns)
    first_shape = inverse.shape[1:] if phases > 1 else (16, LANES)
    stack, *odd = pl.pallas_call(
        functools.partial(correlate_kernel, groups, columns, phases, entries, windows, scale),
        out_shape=outs,
        in_specs=[anywhere] * 6,
        out_specs=[vmem] * len(outs),
        scratch_shapes=[
            pltpu.SMEM((1, 2, entries), jnp.int32),
            pltpu.SMEM((1, entries), jnp.int32),
            pltpu.VMEM((windows, channels), jnp.int32),
            pltpu.VMEM((lanes, NFFT), bf16),
            pltpu.VMEM(first_shape, bf16),
            pltpu.VMEM((CAP * BLK, depth), bf16),
            pltpu.VMEM((tiles, tile_rows, NFFT), bf16),
            pltpu.VMEM((groups, phases, columns, rows, lanes), bf16),
            pltpu.VMEM((8, LANES), jnp.int32),
            pltpu.VMEM((columns, 8, LANES), jnp.int32),
            pltpu.SMEM((columns, 8, LANES), jnp.int32),
            pltpu.SMEM((2, groups * CAP), jnp.int32),
        ]
        + [pltpu.VMEM((devices, rows, lanes), bf16) for _ in range(phases)]
        + [pltpu.VMEM((columns - 1, entries, rows, BLK), bf16) for _ in range(phases)]
        + [pltpu.VMEM((groups - 1, columns, CAP, rows, BLK), bf16) for _ in range(phases)]
        + [pltpu.VMEM((entries, rows, BLK), bf16) for _ in range(phases * columns)]
        + [pltpu.VMEM(stack_shape, bf16) for _ in range(phases - 1)]
        + [dma((4,)), dma((1,)), dma((tiles,)), dma((2,)), dma((columns,)), dma((columns,))]
        + [dma((phases,)) for _ in range(4)]
        + [dma((phases, columns)), dma((phases,)), dma((phases, groups))],
        compiler_params=pltpu.CompilerParams(
            collective_id=0, has_side_effects=True, vmem_limit_bytes=44 * 1024 * 1024
        ),
    )(
        *[
            pltpu.with_memory_space_constraint(operand, pltpu.HBM)
            for operand in (
                pair_list.transpose(0, 2, 1),
                owner_group,
                valid_mask,
                strain.reshape(lanes, NFFT),
                jnp.asarray(forward_rows(groups, columns)).reshape(tiles, tile_rows, NFFT),
                jnp.asarray(inverse[0] if phases > 1 else np.zeros(first_shape, bf16)),
            )
        ]
    )
    if phases > 1:
        stacked = pl.pallas_call(
            lags_kernel,
            out_shape=jax.ShapeDtypeStruct((CAP * BLK, NFFT), jnp.float32),
            in_specs=[vmem] * 3,
            out_specs=anywhere,
            scratch_shapes=[
                pltpu.VMEM((CAP * BLK, depth), bf16),
                pltpu.VMEM((CAP * BLK, NFFT), jnp.float32),
                dma((2, NFFT // 2 // LAGS)),
            ],
            compiler_params=pltpu.CompilerParams(vmem_limit_bytes=44 * 1024 * 1024),
        )(stack, odd[0], jnp.asarray(inverse[1]))
    else:
        stacked = jnp.einsum(
            "skr,kt->srt",
            stack.reshape(CAP, depth, BLK),
            jnp.asarray(inverse[0]),
            preferred_element_type=jnp.float32,
        )
    return stacked.reshape(1, 1, CAP, BLK, NFFT)


def solution(mesh):
    placed = (P("grp", "ch", None), P("grp", "ch"), P("ch", None, None), P("ch", None))
    return jax.shard_map(
        local,
        mesh=mesh,
        in_specs=placed,
        out_specs=P("grp", "ch", None, None, None),
        check_vma=False,
    )
```

```python
import functools
import math

import jax
import jax.numpy as jnp
import numpy as np
from jax import lax
from jax.experimental import pallas as pl
from jax.experimental.pallas import tpu as pltpu
from jax.sharding import PartitionSpec as P

NFFT = 4096
NB = 1024
SUB = 64
BLK = 128
CAP = 2
LANES = 128
UNIT = 8
LAGS = 512
MESH = pl.DeviceIdType.MESH


def phases_of(devices):
    return 2 if NB // devices % (2 * UNIT) == 0 else 1


def bin_numbers(groups, columns):
    phases = phases_of(groups * columns)
    tile_bins = columns * UNIT * phases
    bins = 1 + np.arange(NB, dtype=np.int64)
    bins = bins.reshape(groups, NB // tile_bins // groups, columns, UNIT, phases)
    return bins.transpose(0, 1, 4, 2, 3)


def table_rows(bins, samples, taper):
    angles = np.mod(bins[..., None, :, None] * samples, NFFT) * (2.0 * math.pi / NFFT)
    rows = np.concatenate([np.cos(angles), -np.sin(angles)], axis=-3) * taper
    return rows.reshape(2 * bins.size, len(samples)).astype(jnp.bfloat16)


@functools.lru_cache(maxsize=None)
def forward_rows(groups, columns):
    samples = np.arange(NFFT, dtype=np.int64)
    taper = 0.5 - 0.5 * np.cos(samples * (2.0 * math.pi / NFFT))
    return table_rows(bin_numbers(groups, columns), samples, taper)


@functools.lru_cache(maxsize=None)
def inverse_rows(groups, columns):
    phases = phases_of(groups * columns)
    bins = bin_numbers(groups, columns).transpose(2, 1, 0, 3, 4)
    samples = np.arange(NFFT, dtype=np.int64) - NFFT // 2
    if phases > 1:
        samples = samples[NFFT // 2 :]
    rows = table_rows(bins, samples, np.ones(len(samples)))
    return rows.reshape(phases, 2 * NB // phases, len(samples))


def loop(low, high, body):
    def step_body(step, carry):
        body(step)
        return carry

    lax.fori_loop(low, high, step_body, 0)


def transposed(stack_refs, left_ref):
    for place, stack_ref in enumerate(stack_refs):
        depth = stack_ref.shape[1] * stack_ref.shape[2]
        for rank in range(CAP):
            block = stack_ref[rank].reshape(depth, BLK).astype(jnp.float32)
            rows = slice(rank * BLK, (rank + 1) * BLK)
            left_ref[rows, place * depth : (place + 1) * depth] = block.T.astype(jnp.bfloat16)


def list_row(groups, entries, pairs_ref, owners_ref):
    lane = lax.broadcasted_iota(jnp.int32, (8, LANES), 1)
    row = jnp.zeros((8, LANES), jnp.int32)
    for entry in range(entries):
        owner = owners_ref[0, entry]
        rank = jnp.int32(0)
        for before in range(entry):
            rank += (owners_ref[0, before] == owner).astype(jnp.int32)
        base = 2 * entries + 4 * (owner * CAP + rank)
        for side in range(2):
            block = pairs_ref[0, side, entry]
            row = jnp.where((lane == 2 * entry + side) | (lane == base + side), block, row)
        row = jnp.where(lane == base + 2, 1, row)
        row = jnp.where(lane == base + 3, entry, row)
    return row


def correlate_kernel(
    groups, columns, phases, entries, windows, scale,
    pairs_hbm, owners_hbm, mask_hbm, strain_hbm, table_hbm, inverse_hbm, *rest,
):
    per_group = table_hbm.shape[0] // groups
    subs = phases * per_group
    hops = subs - 1
    last = subs - per_group if phases > 1 else 0
    rest = list(rest)
    take = lambda count: [rest.pop(0) for _ in range(count)]
    out_stacks = take(subs - last)
    odd_ref = take(1)[0] if phases > 1 else None
    pairs_ref, owners_ref, mask_ref, strain_ref, inverse_buf, left_buf = take(6)
    table_buf, white_buf, list_buf, lists_buf, lists_smem, slot_buf = take(6)
    rows_bufs, swap_bufs, forward_bufs = take(phases), take(hops), take(hops)
    entry_bufs = [take(columns) for _ in range(hops)]
    stack_bufs = take(last) + out_stacks
    in_sem, inverse_sem, table_sem, own_sem, lsend_sem, lrecv_sem = take(6)
    wown_sem, wsend_sem, wrecv_sem, hsend_sem, hrecv_sem, fsend_sem, frecv_sem = take(7)
    ssend_sem, srecv_sem = take(2)
    devices = groups * columns
    my_group = lax.axis_index("grp")
    mine = lax.axis_index("ch")
    me = my_group * columns + mine
    tiles = table_buf.shape[0]
    unit_rows = 2 * UNIT

    def group_at(index):
        return lax.rem(index + my_group, groups)

    def tile_copy(index):
        place = group_at(index // per_group) * per_group + lax.rem(index, per_group)
        return pltpu.make_async_copy(
            table_hbm.at[place], table_buf.at[index], table_sem.at[index]
        )

    inputs = [
        pltpu.make_async_copy(source, target, in_sem.at[place])
        for place, (source, target) in enumerate(
            [
                (pairs_hbm, pairs_ref),
                (owners_hbm, owners_ref),
                (mask_hbm, mask_ref),
                (strain_hbm, strain_ref),
            ]
        )
    ]
    inputs[3].start()
    tile_copy(0).start()
    for copy in inputs[:3]:
        copy.start()
    barrier = pltpu.get_barrier_semaphore()

    def greet(step):
        column = lax.rem(mine + step, columns)
        for other in range(groups):
            group = group_at(other)
            if other == 0:

                @pl.when(step > 0)
                def _():
                    pl.semaphore_signal(
                        barrier, inc=1, device_id=(group, column), device_id_type=MESH
                    )

            else:
                pl.semaphore_signal(
                    barrier, inc=1, device_id=(group, column), device_id_type=MESH
                )

    loop(0, columns, greet)
    loop(1, tiles, lambda index: tile_copy(index).start())
    if phases > 1:
        inverse_copy = pltpu.make_async_copy(inverse_hbm, inverse_buf, inverse_sem.at[0])
        inverse_copy.start()
    for copy in inputs:
        copy.wait()
    list_buf[...] = list_row(groups, entries, pairs_ref, owners_ref)

    def compute_tile(index):
        tile_copy(index).wait()
        spectrum = lax.dot_general(
            table_buf[index],
            strain_ref[...],
            (((1,), (1,)), ((), ())),
            preferred_element_type=jnp.float32,
        )
        lanes = spectrum.shape[1]
        parts = spectrum.reshape(phases, columns, 2, UNIT, lanes)
        power = parts[:, :, 0] * parts[:, :, 0] + parts[:, :, 1] * parts[:, :, 1]
        bands = phases * columns * UNIT // SUB
        power = power.reshape(phases, bands, columns // bands, UNIT, lanes)
        power = jnp.sum(jnp.sum(power, axis=2), axis=0)
        band_power = jnp.sum(power, axis=1, keepdims=True) / SUB
        usable = jnp.concatenate([mask_ref[w : w + 1, :] for w in range(windows)], axis=1)
        gain = usable.astype(jnp.float32).reshape(1, 1, lanes) / jnp.sqrt(band_power + 1e-06)
        gain = gain.reshape(1, bands, 1, 1, lanes)
        white = parts.reshape(phases, bands, columns // bands, unit_rows, lanes) * gain
        white = white.reshape(phases, columns, unit_rows, lanes).astype(jnp.bfloat16)
        at = pl.ds(pl.multiple_of(lax.rem(index, per_group) * unit_rows, unit_rows), unit_rows)
        white_buf[index // per_group, :, :, at, :] = white

    def white_copy(phase, index, column):
        return pltpu.make_async_remote_copy(
            src_ref=white_buf.at[index, phase, column],
            dst_ref=rows_bufs[phase].at[me],
            send_sem=wsend_sem.at[phase],
            recv_sem=wrecv_sem.at[phase],
            device_id=(group_at(index), column),
            device_id_type=MESH,
        )

    def white_own(phase):
        return pltpu.make_async_copy(
            white_buf.at[0, phase, mine], rows_bufs[phase].at[me], wown_sem.at[phase]
        )

    def send_white(phase, index):
        def send(step):
            white_copy(phase, index, lax.rem(mine + step, columns)).start()

        loop(1, columns, send)
        if isinstance(index, int) and index == 0:
            white_own(phase).start()
        else:
            send(0)

    def list_copy(step):
        return pltpu.make_async_remote_copy(
            src_ref=list_buf,
            dst_ref=lists_buf.at[mine],
            send_sem=lsend_sem.at[step],
            recv_sem=lrecv_sem.at[step],
            device_id=(my_group, lax.rem(mine + step, columns)),
            device_id_type=MESH,
        )

    loop(0, per_group, compute_tile)
    pl.semaphore_wait(barrier, devices - 1)
    send_white(0, 0)
    loop(1, columns, lambda step: list_copy(step).start())
    own_list = pltpu.make_async_copy(list_buf, lists_buf.at[mine], own_sem.at[0])
    own_list.start()

    def compute_and_send(index):
        loop(index * per_group, (index + 1) * per_group, compute_tile)
        send_white(0, index)

    loop(1, groups, compute_and_send)
    for phase in range(1, phases):
        send_white(phase, 0)
        loop(1, groups, lambda index, phase=phase: send_white(phase, index))

    own_list.wait()
    loop(1, columns, lambda step: list_copy(step).wait())
    to_smem = pltpu.make_async_copy(lists_buf, lists_smem, own_sem.at[1])
    to_smem.start()
    to_smem.wait()

    def cross(sub, first, second):
        rows_ref = rows_bufs[sub // per_group]
        unit = pl.ds(sub % per_group * unit_rows, unit_rows)
        real = jnp.zeros((UNIT, BLK), jnp.float32)
        imag = jnp.zeros((UNIT, BLK), jnp.float32)
        for group in range(groups):
            a = rows_ref[group * columns + first, unit].astype(jnp.float32)
            b = rows_ref[group * columns + second, unit].astype(jnp.float32)
            for window in range(windows):
                lanes = slice(window * BLK, (window + 1) * BLK)
                a_real, a_imag = a[:UNIT, lanes], a[UNIT:, lanes]
                b_real, b_imag = b[:UNIT, lanes], b[UNIT:, lanes]
                real += a_real * b_real + a_imag * b_imag
                imag += a_real * b_imag - a_imag * b_real
        return jnp.concatenate([real, imag], axis=0) * scale

    def cross_entries(sub, column, out_ref):
        for entry in range(entries):
            first = lists_smem[column, 0, 2 * entry]
            second = lists_smem[column, 0, 2 * entry + 1]
            out_ref[entry] = cross(sub, first, second).astype(jnp.bfloat16)

    def slot_lane(slot, place):
        return 2 * entries + 4 * slot + place

    def cross_slots(sub, column):
        for group in range(groups):
            for rank in range(CAP):
                slot = group * CAP + rank
                first = lists_smem[column, 0, slot_lane(slot, 0)]
                second = lists_smem[column, 0, slot_lane(slot, 1)]
                used = lists_smem[column, 0, slot_lane(slot, 2)].astype(jnp.float32)
                block = cross(sub, first, second) * used
                slot_buf[group, column, rank] = block.astype(jnp.bfloat16)

    def swap_copy(sub, step):
        return pltpu.make_async_remote_copy(
            src_ref=swap_bufs[sub].at[step - 1],
            dst_ref=entry_bufs[sub][step],
            send_sem=hsend_sem.at[sub, step],
            recv_sem=hrecv_sem.at[sub, step],
            device_id=(my_group, lax.rem(mine + step, columns)),
            device_id_type=MESH,
        )

    def forward_copy(sub, other, source):
        return pltpu.make_async_remote_copy(
            src_ref=forward_bufs[sub].at[other - 1, source],
            dst_ref=stack_bufs[sub].at[:, my_group * columns + source],
            send_sem=fsend_sem.at[sub],
            recv_sem=frecv_sem.at[sub, my_group],
            device_id=(group_at(other), mine),
            device_id_type=MESH,
        )

    def slot_copy(group, column):
        return pltpu.make_async_remote_copy(
            src_ref=slot_buf.at[group, column],
            dst_ref=stack_bufs[hops].at[:, me],
            send_sem=ssend_sem.at[0],
            recv_sem=srecv_sem.at[0],
            device_id=(group, column),
            device_id_type=MESH,
        )

    slot_own = pltpu.make_async_copy(
        slot_buf.at[my_group, mine], stack_bufs[hops].at[:, me], own_sem.at[2]
    )

    def arrived(ref, sem):
        return pltpu.make_async_remote_copy(
            src_ref=ref,
            dst_ref=ref,
            send_sem=sem,
            recv_sem=sem,
            device_id=(lax.rem(my_group + 1, groups), mine),
            device_id_type=MESH,
        )

    def forward(sub, step):
        source = lax.rem(mine - step + columns, columns)
        if step > 0:
            swap_copy(sub, step).wait_recv()
        for other in range(groups):
            for rank in range(CAP):
                slot = group_at(other) * CAP + rank
                used = lists_smem[mine, 0, slot_lane(slot, 2)].astype(jnp.float32)
                entry = lists_smem[mine, 0, slot_lane(slot, 3)]
                block = (entry_bufs[sub][step][entry].astype(jnp.float32) * used).astype(jnp.bfloat16)
                if other == 0:
                    stack_bufs[sub][rank, my_group * columns + source] = block
                else:
                    forward_bufs[sub][other - 1, source, rank] = block
            if other > 0:
                forward_copy(sub, other, source).start()

    def after_cross(sub, step):
        if 0 < sub and 0 < step:
            swap_copy(sub - 1, step).wait_send()
        if sub < hops and 0 < step:
            swap_copy(sub, step).start()
        if 0 < sub:
            forward(sub - 1, step)

    def each_step(sub, first, step):
        for place in range(first, columns):

            @pl.when(step == place)
            def _():
                after_cross(sub, place)

    def cross_sub(sub):
        if sub % per_group == 0:
            phase = sub // per_group
            white_own(phase).wait()
            arrived(rows_bufs[phase].at[pl.ds(0, devices - 1)], wrecv_sem.at[phase]).wait_recv()
        if sub < hops:

            def entries_step(step):
                cross_entries(sub, lax.rem(mine + step, columns), swap_bufs[sub].at[step - 1])
                each_step(sub, 1, step)

            loop(1, columns, entries_step)
            cross_entries(sub, mine, entry_bufs[sub][0])
            after_cross(sub, 0)
        else:

            def slots_step(step):
                column = lax.rem(mine + step, columns)
                cross_slots(sub, column)
                for other in range(groups):
                    group = group_at(other)
                    if other > 0:
                        slot_copy(group, column).start()
                    else:

                        @pl.when(step < columns)
                        def _():
                            slot_copy(group, column).start()

                        @pl.when(step == columns)
                        def _():
                            slot_own.start()

                if 0 < sub:
                    each_step(sub, 1, step)

                    @pl.when(step == columns)
                    def _():
                        after_cross(sub, 0)

            loop(1, columns + 1, slots_step)

    def wait_stack(sub):
        def wait(other):
            group = group_at(other)
            part = stack_bufs[sub].at[:, pl.ds(group * columns, columns)]
            arrived(part, frecv_sem.at[sub, group]).wait_recv()

        loop(1, groups, wait)

    for sub in range(subs):
        cross_sub(sub)
    for sub in range(last):
        wait_stack(sub)
    if last > 0:
        inverse_copy.wait()
        transposed(stack_bufs[:last], left_buf)

        def odd_lags(tile):
            at = pl.ds(pl.multiple_of(tile * LAGS, LAGS), LAGS)
            odd_ref[:, at] = jnp.dot(
                left_buf[...], inverse_buf[:, at], preferred_element_type=jnp.float32
            )

        loop(0, NFFT // 2 // LAGS, odd_lags)
    for phase in range(phases):
        arrived(rows_bufs[phase].at[pl.ds(0, devices - 1)], wsend_sem.at[phase]).wait_send()
    for sub in range(hops):
        arrived(forward_bufs[sub], fsend_sem.at[sub]).wait_send()
    for sub in range(last, hops):
        wait_stack(sub)
    others = stack_bufs[hops].at[:, pl.ds(0, devices - 1)]
    arrived(others, ssend_sem.at[0]).wait_send()
    slot_own.wait()
    arrived(others, srecv_sem.at[0]).wait_recv()


def lags_kernel(*refs):
    stack_refs = refs[:-6]
    odd_ref, inverse_ref, out_hbm, left_buf, out_buf, out_sem = refs[-6:]
    transposed(stack_refs, left_buf)
    count = NFFT // 2 // LAGS

    def copies(tile):
        for side in range(2):
            at = pl.ds(side * (NFFT // 2) + tile * LAGS, LAGS)
            yield pltpu.make_async_copy(
                out_buf.at[:, at], out_hbm.at[:, at], out_sem.at[side, tile]
            )

    for tile in range(count):
        at = slice(tile * LAGS, (tile + 1) * LAGS)
        upper = slice(NFFT // 2 + tile * LAGS, NFFT // 2 + (tile + 1) * LAGS)
        even = jnp.dot(left_buf[...], inverse_ref[:, at], preferred_element_type=jnp.float32)
        odd = odd_ref[:, at]
        out_buf[:, at] = even - odd
        out_buf[:, upper] = even + odd
        for copy in copies(tile):
            copy.start()
    for tile in range(count):
        for copy in copies(tile):
            copy.wait()


def local(strain, valid_mask, pair_list, owner_group):
    windows, channels = valid_mask.shape
    groups = lax.axis_size("grp")
    columns = lax.axis_size("ch")
    devices = groups * columns
    entries = owner_group.shape[1]
    phases = phases_of(devices)
    rows = 2 * NB // devices // phases
    lanes = windows * channels
    tiles = NB // (columns * UNIT * phases)
    tile_rows = 2 * NB // tiles
    scale = 1.0 / math.sqrt(NB * windows * groups)

    vmem = pl.BlockSpec(memory_space=pltpu.VMEM)
    anywhere = pl.BlockSpec(memory_space=pltpu.HBM)
    dma = pltpu.SemaphoreType.DMA
    bf16 = jnp.bfloat16
    depth = devices * rows
    per_group = tiles // groups
    subs = phases * per_group
    hops = subs - 1
    last = subs - per_group if phases > 1 else 0
    unit_rows = 2 * UNIT
    stack_shape = (CAP, devices, unit_rows, BLK)
    outs = [jax.ShapeDtypeStruct(stack_shape, bf16) for _ in range(subs - last)]
    if phases > 1:
        outs.append(jax.ShapeDtypeStruct((CAP * BLK, NFFT // 2), jnp.float32))
    inverse = inverse_rows(groups, columns)
    first_shape = inverse.shape[1:] if phases > 1 else (16, LANES)
    stacks = pl.pallas_call(
        functools.partial(correlate_kernel, groups, columns, phases, entries, windows, scale),
        out_shape=outs,
        in_specs=[anywhere] * 6,
        out_specs=[vmem] * len(outs),
        scratch_shapes=[
            pltpu.SMEM((1, 2, entries), jnp.int32),
            pltpu.SMEM((1, entries), jnp.int32),
            pltpu.VMEM((windows, channels), jnp.int32),
            pltpu.VMEM((lanes, NFFT), bf16),
            pltpu.VMEM(first_shape, bf16),
            pltpu.VMEM((CAP * BLK, depth), bf16),
            pltpu.VMEM((tiles, tile_rows, NFFT), bf16),
            pltpu.VMEM((groups, phases, columns, rows, lanes), bf16),
            pltpu.VMEM((8, LANES), jnp.int32),
            pltpu.VMEM((columns, 8, LANES), jnp.int32),
            pltpu.SMEM((columns, 8, LANES), jnp.int32),
            pltpu.VMEM((groups, columns, CAP, unit_rows, BLK), bf16),
        ]
        + [pltpu.VMEM((devices, rows, lanes), bf16) for _ in range(phases)]
        + [pltpu.VMEM((columns - 1, entries, unit_rows, BLK), bf16) for _ in range(hops)]
        + [pltpu.VMEM((groups - 1, columns, CAP, unit_rows, BLK), bf16) for _ in range(hops)]
        + [pltpu.VMEM((entries, unit_rows, BLK), bf16) for _ in range(hops * columns)]
        + [pltpu.VMEM(stack_shape, bf16) for _ in range(last)]
        + [dma((4,)), dma((1,)), dma((tiles,)), dma((3,)), dma((columns,)), dma((columns,))]
        + [dma((phases,)), dma((phases,)), dma((phases,))]
        + [dma((max(1, hops), columns)), dma((max(1, hops), columns))]
        + [dma((max(1, hops),)), dma((max(1, hops), groups)), dma((1,)), dma((1,))],
        compiler_params=pltpu.CompilerParams(
            collective_id=0, has_side_effects=True, vmem_limit_bytes=44 * 1024 * 1024
        ),
    )(
        *[
            pltpu.with_memory_space_constraint(operand, pltpu.HBM)
            for operand in (
                pair_list.transpose(0, 2, 1),
                owner_group,
                valid_mask,
                strain.reshape(lanes, NFFT),
                jnp.asarray(forward_rows(groups, columns)).reshape(tiles, tile_rows, NFFT),
                jnp.asarray(inverse[0] if phases > 1 else np.zeros(first_shape, bf16)),
            )
        ]
    )
    if phases > 1:
        stacked = pl.pallas_call(
            lags_kernel,
            out_shape=jax.ShapeDtypeStruct((CAP * BLK, NFFT), jnp.float32),
            in_specs=[vmem] * (len(outs) + 1),
            out_specs=anywhere,
            scratch_shapes=[
                pltpu.VMEM((CAP * BLK, depth), bf16),
                pltpu.VMEM((CAP * BLK, NFFT), jnp.float32),
                dma((2, NFFT // 2 // LAGS)),
            ],
            compiler_params=pltpu.CompilerParams(vmem_limit_bytes=44 * 1024 * 1024),
        )(*stacks, jnp.asarray(inverse[1]))
    else:
        stacked = jnp.einsum(
            "skr,kt->srt",
            stacks[0].reshape(CAP, depth, BLK),
            jnp.asarray(inverse[0]),
            preferred_element_type=jnp.float32,
        )
    return stacked.reshape(1, 1, CAP, BLK, NFFT)


def solution(mesh):
    placed = (P("grp", "ch", None), P("grp", "ch"), P("ch", None, None), P("ch", None))
    return jax.shard_map(
        local,
        mesh=mesh,
        in_specs=placed,
        out_specs=P("grp", "ch", None, None, None),
        check_vma=False,
    )
```

```python
import functools
import math

import jax
import jax.numpy as jnp
import numpy as np
from jax import lax
from jax.experimental import pallas as pl
from jax.experimental.pallas import tpu as pltpu
from jax.sharding import PartitionSpec as P

NFFT = 4096
NB = 1024
SUB = 64
BLK = 128
CAP = 2
LANES = 128
UNIT = 8
LAGS = 512
AHEAD = 3
MESH = pl.DeviceIdType.MESH


def phases_of(devices):
    return 2 if NB // devices % (2 * UNIT) == 0 else 1


def bin_numbers(groups, columns):
    phases = phases_of(groups * columns)
    tile_bins = columns * UNIT * phases
    bins = 1 + np.arange(NB, dtype=np.int64)
    bins = bins.reshape(groups, NB // tile_bins // groups, columns, UNIT, phases)
    return bins.transpose(0, 1, 4, 2, 3)


def table_rows(bins, samples, taper):
    angles = np.mod(bins[..., None, :, None] * samples, NFFT) * (2.0 * math.pi / NFFT)
    rows = np.concatenate([np.cos(angles), -np.sin(angles)], axis=-3) * taper
    return rows.reshape(2 * bins.size, len(samples)).astype(jnp.bfloat16)


@functools.lru_cache(maxsize=None)
def forward_rows(groups, columns):
    samples = np.arange(NFFT, dtype=np.int64)
    taper = 0.5 - 0.5 * np.cos(samples * (2.0 * math.pi / NFFT))
    return table_rows(bin_numbers(groups, columns), samples, taper)


@functools.lru_cache(maxsize=None)
def inverse_rows(groups, columns):
    phases = phases_of(groups * columns)
    bins = bin_numbers(groups, columns).transpose(2, 1, 0, 3, 4)
    samples = np.arange(NFFT, dtype=np.int64) - NFFT // 2
    if phases > 1:
        samples = samples[NFFT // 2 :]
    rows = table_rows(bins, samples, np.ones(len(samples)))
    return rows.reshape(phases, 2 * NB // phases, len(samples))


def loop(low, high, body):
    def step_body(step, carry):
        body(step)
        return carry

    lax.fori_loop(low, high, step_body, 0)


def transposed(stack_refs, left_ref):
    for place, stack_ref in enumerate(stack_refs):
        depth = stack_ref.shape[1] * stack_ref.shape[2]
        for rank in range(CAP):
            block = stack_ref[rank].reshape(depth, BLK).astype(jnp.float32)
            rows = slice(rank * BLK, (rank + 1) * BLK)
            left_ref[rows, place * depth : (place + 1) * depth] = block.T.astype(jnp.bfloat16)


def list_row(groups, entries, pairs_ref, owners_ref):
    lane = lax.broadcasted_iota(jnp.int32, (8, LANES), 1)
    row = jnp.zeros((8, LANES), jnp.int32)
    for entry in range(entries):
        owner = owners_ref[0, entry]
        rank = jnp.int32(0)
        for before in range(entry):
            rank += (owners_ref[0, before] == owner).astype(jnp.int32)
        base = 2 * entries + 4 * (owner * CAP + rank)
        for side in range(2):
            block = pairs_ref[0, side, entry]
            row = jnp.where((lane == 2 * entry + side) | (lane == base + side), block, row)
        row = jnp.where(lane == base + 2, 1, row)
        row = jnp.where(lane == base + 3, entry, row)
    return row


def correlate_kernel(
    groups, columns, phases, entries, windows, scale,
    pairs_hbm, owners_hbm, mask_hbm, strain_hbm, table_hbm, inverse_hbm, *rest,
):
    per_group = table_hbm.shape[0] // groups
    subs = phases * per_group
    hops = subs - 1
    last = subs - per_group if phases > 1 else 0
    rest = list(rest)
    take = lambda count: [rest.pop(0) for _ in range(count)]
    out_stacks = take(subs - last)
    odd_ref, later_ref = take(2) if phases > 1 else (None, None)
    pairs_ref, owners_ref, mask_ref, strain_ref, inverse_buf, left_buf = take(6)
    table_buf, white_buf, list_buf, lists_buf, lists_smem, slot_buf = take(6)
    rows_bufs, swap_bufs, forward_bufs = take(phases), take(hops), take(hops)
    entry_bufs = [take(columns) for _ in range(hops)]
    stack_bufs = take(last) + out_stacks
    in_sem, inverse_sem, table_sem, own_sem, lsend_sem, lrecv_sem = take(6)
    wown_sem, wsend_sem, wrecv_sem, hsend_sem, hrecv_sem, fsend_sem, frecv_sem = take(7)
    ssend_sem, srecv_sem = take(2)
    devices = groups * columns
    my_group = lax.axis_index("grp")
    mine = lax.axis_index("ch")
    me = my_group * columns + mine
    tiles = table_buf.shape[0]
    unit_rows = 2 * UNIT

    def group_at(index):
        return lax.rem(index + my_group, groups)

    def tile_copy(index):
        place = group_at(index // per_group) * per_group + lax.rem(index, per_group)
        return pltpu.make_async_copy(
            table_hbm.at[place], table_buf.at[index], table_sem.at[index]
        )

    inputs = [
        pltpu.make_async_copy(source, target, in_sem.at[place])
        for place, (source, target) in enumerate(
            [
                (pairs_hbm, pairs_ref),
                (owners_hbm, owners_ref),
                (mask_hbm, mask_ref),
                (strain_hbm, strain_ref),
            ]
        )
    ]
    inputs[3].start()
    tile_copy(0).start()
    for copy in inputs[:3]:
        copy.start()
    barrier = pltpu.get_barrier_semaphore()

    def greet(step):
        column = lax.rem(mine + step, columns)
        for other in range(groups):
            group = group_at(other)
            if other == 0:

                @pl.when(step > 0)
                def _():
                    pl.semaphore_signal(
                        barrier, inc=1, device_id=(group, column), device_id_type=MESH
                    )

            else:
                pl.semaphore_signal(
                    barrier, inc=1, device_id=(group, column), device_id_type=MESH
                )

    loop(0, columns, greet)
    loop(1, min(AHEAD, tiles), lambda index: tile_copy(index).start())
    for copy in inputs:
        copy.wait()
    list_buf[...] = list_row(groups, entries, pairs_ref, owners_ref)

    def compute_tile(index):
        @pl.when(index + AHEAD < tiles)
        def _():
            tile_copy(index + AHEAD).start()

        tile_copy(index).wait()
        spectrum = lax.dot_general(
            table_buf[index],
            strain_ref[...],
            (((1,), (1,)), ((), ())),
            preferred_element_type=jnp.float32,
        )
        lanes = spectrum.shape[1]
        parts = spectrum.reshape(phases, columns, 2, UNIT, lanes)
        power = parts[:, :, 0] * parts[:, :, 0] + parts[:, :, 1] * parts[:, :, 1]
        bands = phases * columns * UNIT // SUB
        power = power.reshape(phases, bands, columns // bands, UNIT, lanes)
        power = jnp.sum(jnp.sum(power, axis=2), axis=0)
        band_power = jnp.sum(power, axis=1, keepdims=True) / SUB
        usable = jnp.concatenate([mask_ref[w : w + 1, :] for w in range(windows)], axis=1)
        gain = usable.astype(jnp.float32).reshape(1, 1, lanes) / jnp.sqrt(band_power + 1e-06)
        gain = gain.reshape(1, bands, 1, 1, lanes)
        white = parts.reshape(phases, bands, columns // bands, unit_rows, lanes) * gain
        white = white.reshape(phases, columns, unit_rows, lanes).astype(jnp.bfloat16)
        at = pl.ds(pl.multiple_of(lax.rem(index, per_group) * unit_rows, unit_rows), unit_rows)
        white_buf[index // per_group, :, :, at, :] = white

    def white_copy(phase, index, column):
        return pltpu.make_async_remote_copy(
            src_ref=white_buf.at[index, phase, column],
            dst_ref=rows_bufs[phase].at[me],
            send_sem=wsend_sem.at[phase],
            recv_sem=wrecv_sem.at[phase],
            device_id=(group_at(index), column),
            device_id_type=MESH,
        )

    def white_own(phase):
        return pltpu.make_async_copy(
            white_buf.at[0, phase, mine], rows_bufs[phase].at[me], wown_sem.at[phase]
        )

    def send_white(phase, index):
        def send(step):
            white_copy(phase, index, lax.rem(mine + step, columns)).start()

        loop(1, columns, send)
        if isinstance(index, int) and index == 0:
            white_own(phase).start()
        else:
            send(0)

    def list_copy(step):
        return pltpu.make_async_remote_copy(
            src_ref=list_buf,
            dst_ref=lists_buf.at[mine],
            send_sem=lsend_sem.at[step],
            recv_sem=lrecv_sem.at[step],
            device_id=(my_group, lax.rem(mine + step, columns)),
            device_id_type=MESH,
        )

    loop(0, per_group, compute_tile)
    pl.semaphore_wait(barrier, devices - 1)
    send_white(0, 0)
    loop(1, columns, lambda step: list_copy(step).start())
    own_list = pltpu.make_async_copy(list_buf, lists_buf.at[mine], own_sem.at[0])
    own_list.start()

    def compute_and_send(index):
        loop(index * per_group, (index + 1) * per_group, compute_tile)
        send_white(0, index)

    loop(1, groups, compute_and_send)
    if phases > 1:
        inverse_copies = [
            pltpu.make_async_copy(inverse_hbm.at[place], target, inverse_sem.at[place])
            for place, target in enumerate([inverse_buf, later_ref])
        ]
        for copy in inverse_copies:
            copy.start()
    for phase in range(1, phases):
        send_white(phase, 0)
        loop(1, groups, lambda index, phase=phase: send_white(phase, index))

    own_list.wait()
    loop(1, columns, lambda step: list_copy(step).wait())
    to_smem = pltpu.make_async_copy(lists_buf, lists_smem, own_sem.at[1])
    to_smem.start()
    to_smem.wait()

    def cross(sub, first, second):
        rows_ref = rows_bufs[sub // per_group]
        unit = pl.ds(sub % per_group * unit_rows, unit_rows)
        real = jnp.zeros((UNIT, BLK), jnp.float32)
        imag = jnp.zeros((UNIT, BLK), jnp.float32)
        for group in range(groups):
            a = rows_ref[group * columns + first, unit].astype(jnp.float32)
            b = rows_ref[group * columns + second, unit].astype(jnp.float32)
            for window in range(windows):
                lanes = slice(window * BLK, (window + 1) * BLK)
                a_real, a_imag = a[:UNIT, lanes], a[UNIT:, lanes]
                b_real, b_imag = b[:UNIT, lanes], b[UNIT:, lanes]
                real += a_real * b_real + a_imag * b_imag
                imag += a_real * b_imag - a_imag * b_real
        return jnp.concatenate([real, imag], axis=0) * scale

    def cross_entries(sub, column, out_ref):
        for entry in range(entries):
            first = lists_smem[column, 0, 2 * entry]
            second = lists_smem[column, 0, 2 * entry + 1]
            out_ref[entry] = cross(sub, first, second).astype(jnp.bfloat16)

    def slot_lane(slot, place):
        return 2 * entries + 4 * slot + place

    def cross_slots(sub, column):
        for group in range(groups):
            for rank in range(CAP):
                slot = group * CAP + rank
                first = lists_smem[column, 0, slot_lane(slot, 0)]
                second = lists_smem[column, 0, slot_lane(slot, 1)]
                used = lists_smem[column, 0, slot_lane(slot, 2)].astype(jnp.float32)
                block = cross(sub, first, second) * used
                slot_buf[group, column, rank] = block.astype(jnp.bfloat16)

    def swap_copy(sub, step):
        return pltpu.make_async_remote_copy(
            src_ref=swap_bufs[sub].at[step - 1],
            dst_ref=entry_bufs[sub][step],
            send_sem=hsend_sem.at[sub, step],
            recv_sem=hrecv_sem.at[sub, step],
            device_id=(my_group, lax.rem(mine + step, columns)),
            device_id_type=MESH,
        )

    def forward_copy(sub, other, source):
        return pltpu.make_async_remote_copy(
            src_ref=forward_bufs[sub].at[other - 1, source],
            dst_ref=stack_bufs[sub].at[:, my_group * columns + source],
            send_sem=fsend_sem.at[sub],
            recv_sem=frecv_sem.at[sub, my_group],
            device_id=(group_at(other), mine),
            device_id_type=MESH,
        )

    def slot_copy(group, column):
        return pltpu.make_async_remote_copy(
            src_ref=slot_buf.at[group, column],
            dst_ref=stack_bufs[hops].at[:, me],
            send_sem=ssend_sem.at[0],
            recv_sem=srecv_sem.at[0],
            device_id=(group, column),
            device_id_type=MESH,
        )

    slot_own = pltpu.make_async_copy(
        slot_buf.at[my_group, mine], stack_bufs[hops].at[:, me], own_sem.at[2]
    )

    def arrived(ref, sem):
        return pltpu.make_async_remote_copy(
            src_ref=ref,
            dst_ref=ref,
            send_sem=sem,
            recv_sem=sem,
            device_id=(lax.rem(my_group + 1, groups), mine),
            device_id_type=MESH,
        )

    def forward(sub, step):
        source = lax.rem(mine - step + columns, columns)
        if step > 0:
            swap_copy(sub, step).wait_recv()
        for other in range(groups):
            for rank in range(CAP):
                slot = group_at(other) * CAP + rank
                used = lists_smem[mine, 0, slot_lane(slot, 2)].astype(jnp.float32)
                entry = lists_smem[mine, 0, slot_lane(slot, 3)]
                block = (entry_bufs[sub][step][entry].astype(jnp.float32) * used).astype(jnp.bfloat16)
                if other == 0:
                    stack_bufs[sub][rank, my_group * columns + source] = block
                else:
                    forward_bufs[sub][other - 1, source, rank] = block
            if other > 0:
                forward_copy(sub, other, source).start()

    def after_cross(sub, step):
        if 0 < sub and 0 < step:
            swap_copy(sub - 1, step).wait_send()
        if sub < hops and 0 < step:
            swap_copy(sub, step).start()
        if 0 < sub:
            forward(sub - 1, step)

    def each_step(sub, first, step):
        for place in range(first, columns):

            @pl.when(step == place)
            def _():
                after_cross(sub, place)

    def cross_sub(sub):
        if sub % per_group == 0:
            phase = sub // per_group
            white_own(phase).wait()
            arrived(rows_bufs[phase].at[pl.ds(0, devices - 1)], wrecv_sem.at[phase]).wait_recv()
        if sub < hops:

            def entries_step(step):
                cross_entries(sub, lax.rem(mine + step, columns), swap_bufs[sub].at[step - 1])
                each_step(sub, 1, step)

            loop(1, columns, entries_step)
            cross_entries(sub, mine, entry_bufs[sub][0])
            after_cross(sub, 0)
        else:

            def slots_step(step):
                column = lax.rem(mine + step, columns)
                cross_slots(sub, column)
                for other in range(groups):
                    group = group_at(other)
                    if other > 0:
                        slot_copy(group, column).start()
                    else:

                        @pl.when(step < columns)
                        def _():
                            slot_copy(group, column).start()

                        @pl.when(step == columns)
                        def _():
                            slot_own.start()

                if 0 < sub:
                    each_step(sub, 1, step)

                    @pl.when(step == columns)
                    def _():
                        after_cross(sub, 0)

            loop(1, columns + 1, slots_step)

    def wait_stack(sub):
        def wait(other):
            group = group_at(other)
            part = stack_bufs[sub].at[:, pl.ds(group * columns, columns)]
            arrived(part, frecv_sem.at[sub, group]).wait_recv()

        loop(1, groups, wait)

    for sub in range(subs):
        cross_sub(sub)
    for sub in range(last):
        wait_stack(sub)
    if last > 0:
        for copy in inverse_copies:
            copy.wait()
        transposed(stack_bufs[:last], left_buf)

        def odd_lags(tile):
            at = pl.ds(pl.multiple_of(tile * LAGS, LAGS), LAGS)
            odd_ref[:, at] = jnp.dot(
                left_buf[...], inverse_buf[:, at], preferred_element_type=jnp.float32
            )

        loop(0, NFFT // 2 // LAGS, odd_lags)
    for phase in range(phases):
        arrived(rows_bufs[phase].at[pl.ds(0, devices - 1)], wsend_sem.at[phase]).wait_send()
    for sub in range(hops):
        arrived(forward_bufs[sub], fsend_sem.at[sub]).wait_send()
    for sub in range(last, hops):
        wait_stack(sub)
    others = stack_bufs[hops].at[:, pl.ds(0, devices - 1)]
    arrived(others, ssend_sem.at[0]).wait_send()
    slot_own.wait()
    arrived(others, srecv_sem.at[0]).wait_recv()


def lags_kernel(*refs):
    stack_refs = refs[:-6]
    odd_ref, inverse_ref, out_hbm, left_buf, out_buf, out_sem = refs[-6:]
    transposed(stack_refs, left_buf)
    count = NFFT // 2 // LAGS

    def copies(tile):
        for side in range(2):
            at = pl.ds(side * (NFFT // 2) + tile * LAGS, LAGS)
            yield pltpu.make_async_copy(
                out_buf.at[:, at], out_hbm.at[:, at], out_sem.at[side, tile]
            )

    for tile in range(count):
        at = slice(tile * LAGS, (tile + 1) * LAGS)
        upper = slice(NFFT // 2 + tile * LAGS, NFFT // 2 + (tile + 1) * LAGS)
        even = jnp.dot(left_buf[...], inverse_ref[:, at], preferred_element_type=jnp.float32)
        odd = odd_ref[:, at]
        out_buf[:, at] = even - odd
        out_buf[:, upper] = even + odd
        for copy in copies(tile):
            copy.start()
    for tile in range(count):
        for copy in copies(tile):
            copy.wait()


def local(strain, valid_mask, pair_list, owner_group):
    windows, channels = valid_mask.shape
    groups = lax.axis_size("grp")
    columns = lax.axis_size("ch")
    devices = groups * columns
    entries = owner_group.shape[1]
    phases = phases_of(devices)
    rows = 2 * NB // devices // phases
    lanes = windows * channels
    tiles = NB // (columns * UNIT * phases)
    tile_rows = 2 * NB // tiles
    scale = 1.0 / math.sqrt(NB * windows * groups)

    vmem = pl.BlockSpec(memory_space=pltpu.VMEM)
    anywhere = pl.BlockSpec(memory_space=pltpu.HBM)
    dma = pltpu.SemaphoreType.DMA
    bf16 = jnp.bfloat16
    depth = devices * rows
    per_group = tiles // groups
    subs = phases * per_group
    hops = subs - 1
    last = subs - per_group if phases > 1 else 0
    unit_rows = 2 * UNIT
    stack_shape = (CAP, devices, unit_rows, BLK)
    outs = [jax.ShapeDtypeStruct(stack_shape, bf16) for _ in range(subs - last)]
    if phases > 1:
        outs.append(jax.ShapeDtypeStruct((CAP * BLK, NFFT // 2), jnp.float32))
        outs.append(jax.ShapeDtypeStruct((NB, NFFT // 2), bf16))
    inverse = inverse_rows(groups, columns)
    first_shape = inverse.shape[1:] if phases > 1 else (16, LANES)
    stacks = pl.pallas_call(
        functools.partial(correlate_kernel, groups, columns, phases, entries, windows, scale),
        out_shape=outs,
        in_specs=[anywhere] * 6,
        out_specs=[vmem] * len(outs),
        scratch_shapes=[
            pltpu.SMEM((1, 2, entries), jnp.int32),
            pltpu.SMEM((1, entries), jnp.int32),
            pltpu.VMEM((windows, channels), jnp.int32),
            pltpu.VMEM((lanes, NFFT), bf16),
            pltpu.VMEM(first_shape, bf16),
            pltpu.VMEM((CAP * BLK, depth), bf16),
            pltpu.VMEM((tiles, tile_rows, NFFT), bf16),
            pltpu.VMEM((groups, phases, columns, rows, lanes), bf16),
            pltpu.VMEM((8, LANES), jnp.int32),
            pltpu.VMEM((columns, 8, LANES), jnp.int32),
            pltpu.SMEM((columns, 8, LANES), jnp.int32),
            pltpu.VMEM((groups, columns, CAP, unit_rows, BLK), bf16),
        ]
        + [pltpu.VMEM((devices, rows, lanes), bf16) for _ in range(phases)]
        + [pltpu.VMEM((columns - 1, entries, unit_rows, BLK), bf16) for _ in range(hops)]
        + [pltpu.VMEM((groups - 1, columns, CAP, unit_rows, BLK), bf16) for _ in range(hops)]
        + [pltpu.VMEM((entries, unit_rows, BLK), bf16) for _ in range(hops * columns)]
        + [pltpu.VMEM(stack_shape, bf16) for _ in range(last)]
        + [dma((4,)), dma((2,)), dma((tiles,)), dma((3,)), dma((columns,)), dma((columns,))]
        + [dma((phases,)), dma((phases,)), dma((phases,))]
        + [dma((max(1, hops), columns)), dma((max(1, hops), columns))]
        + [dma((max(1, hops),)), dma((max(1, hops), groups)), dma((1,)), dma((1,))],
        compiler_params=pltpu.CompilerParams(
            collective_id=0, has_side_effects=True, vmem_limit_bytes=44 * 1024 * 1024
        ),
    )(
        *[
            pltpu.with_memory_space_constraint(operand, pltpu.HBM)
            for operand in (
                pair_list.transpose(0, 2, 1),
                owner_group,
                valid_mask,
                strain.reshape(lanes, NFFT),
                jnp.asarray(forward_rows(groups, columns)).reshape(tiles, tile_rows, NFFT),
                jnp.asarray(inverse if phases > 1 else np.zeros(first_shape, bf16)),
            )
        ]
    )
    if phases > 1:
        stacked = pl.pallas_call(
            lags_kernel,
            out_shape=jax.ShapeDtypeStruct((CAP * BLK, NFFT), jnp.float32),
            in_specs=[vmem] * len(outs),
            out_specs=anywhere,
            scratch_shapes=[
                pltpu.VMEM((CAP * BLK, depth), bf16),
                pltpu.VMEM((CAP * BLK, NFFT), jnp.float32),
                dma((2, NFFT // 2 // LAGS)),
            ],
            compiler_params=pltpu.CompilerParams(vmem_limit_bytes=44 * 1024 * 1024),
        )(*stacks)
    else:
        stacked = jnp.einsum(
            "skr,kt->srt",
            stacks[0].reshape(CAP, depth, BLK),
            jnp.asarray(inverse[0]),
            preferred_element_type=jnp.float32,
        )
    return stacked.reshape(1, 1, CAP, BLK, NFFT)


def solution(mesh):
    placed = (P("grp", "ch", None), P("grp", "ch"), P("ch", None, None), P("ch", None))
    return jax.shard_map(
        local,
        mesh=mesh,
        in_specs=placed,
        out_specs=P("grp", "ch", None, None, None),
        check_vma=False,
    )
```

```python
import functools
import math

import jax
import jax.numpy as jnp
import numpy as np
from jax import lax
from jax.experimental import pallas as pl
from jax.experimental.pallas import tpu as pltpu
from jax.sharding import PartitionSpec as P

NFFT = 4096
NB = 1024
SUB = 64
BLK = 128
CAP = 2
LANES = 128
UNIT = 8
LAGS = 512
AHEAD = 3
WAVES = 2
MESH = pl.DeviceIdType.MESH


def phases_of(devices):
    return 2 if NB // devices % (2 * UNIT) == 0 else 1


def bin_numbers(groups, columns):
    phases = phases_of(groups * columns)
    tile_bins = columns * UNIT * phases
    bins = 1 + np.arange(NB, dtype=np.int64)
    bins = bins.reshape(groups, NB // tile_bins // groups, columns, UNIT, phases)
    return bins.transpose(0, 1, 4, 2, 3)


def table_rows(bins, samples, taper):
    angles = np.mod(bins[..., None, :, None] * samples, NFFT) * (2.0 * math.pi / NFFT)
    rows = np.concatenate([np.cos(angles), -np.sin(angles)], axis=-3) * taper
    return rows.reshape(2 * bins.size, len(samples)).astype(jnp.bfloat16)


@functools.lru_cache(maxsize=None)
def forward_rows(groups, columns):
    samples = np.arange(NFFT, dtype=np.int64)
    taper = 0.5 - 0.5 * np.cos(samples * (2.0 * math.pi / NFFT))
    return table_rows(bin_numbers(groups, columns), samples, taper)


@functools.lru_cache(maxsize=None)
def inverse_rows(groups, columns):
    phases = phases_of(groups * columns)
    bins = bin_numbers(groups, columns).transpose(2, 1, 0, 3, 4)
    samples = np.arange(NFFT, dtype=np.int64) - NFFT // 2
    if phases > 1:
        samples = samples[NFFT // 2 :]
    rows = table_rows(bins, samples, np.ones(len(samples)))
    return rows.reshape(phases, 2 * NB // phases, len(samples))


def loop(low, high, body):
    def step_body(step, carry):
        body(step)
        return carry

    lax.fori_loop(low, high, step_body, 0)


def transposed(stack_refs, left_ref):
    for place, stack_ref in enumerate(stack_refs):
        depth = stack_ref.shape[1] * stack_ref.shape[2]
        for rank in range(CAP):
            block = stack_ref[rank].reshape(depth, BLK).astype(jnp.float32)
            rows = slice(rank * BLK, (rank + 1) * BLK)
            left_ref[rows, place * depth : (place + 1) * depth] = block.T.astype(jnp.bfloat16)


def list_row(groups, entries, pairs_ref, owners_ref):
    lane = lax.broadcasted_iota(jnp.int32, (8, LANES), 1)
    row = jnp.zeros((8, LANES), jnp.int32)
    for entry in range(entries):
        owner = owners_ref[0, entry]
        rank = jnp.int32(0)
        for before in range(entry):
            rank += (owners_ref[0, before] == owner).astype(jnp.int32)
        base = 2 * entries + 4 * (owner * CAP + rank)
        for side in range(2):
            block = pairs_ref[0, side, entry]
            row = jnp.where((lane == 2 * entry + side) | (lane == base + side), block, row)
        row = jnp.where(lane == base + 2, 1, row)
        row = jnp.where(lane == base + 3, entry, row)
    return row


def correlate_kernel(
    groups, columns, phases, entries, windows, scale,
    pairs_hbm, owners_hbm, mask_hbm, strain_hbm, table_hbm, inverse_hbm, *rest,
):
    per_group = table_hbm.shape[0] // groups
    subs = phases * per_group
    hops = subs - 1
    last = subs - per_group if phases > 1 else 0
    rest = list(rest)
    take = lambda count: [rest.pop(0) for _ in range(count)]
    out_stacks = take(subs - last)
    odd_ref, later_ref = take(2) if phases > 1 else (None, None)
    pairs_ref, owners_ref, mask_ref, strain_ref, inverse_buf, left_buf = take(6)
    table_buf, white_buf, list_buf, lists_buf, lists_smem, slot_buf = take(6)
    waves = white_buf.shape[1]
    wave_subs = subs // waves
    rows_bufs, swap_bufs, forward_bufs = take(waves), take(hops), take(hops)
    entry_bufs = [take(columns) for _ in range(hops)]
    stack_bufs = take(last) + out_stacks
    in_sem, inverse_sem, table_sem, own_sem, lsend_sem, lrecv_sem = take(6)
    wown_sem, wsend_sem, wrecv_sem, hsend_sem, hrecv_sem, fsend_sem, frecv_sem = take(7)
    ssend_sem, srecv_sem = take(2)
    devices = groups * columns
    my_group = lax.axis_index("grp")
    mine = lax.axis_index("ch")
    me = my_group * columns + mine
    tiles = table_buf.shape[0]
    unit_rows = 2 * UNIT

    def group_at(index):
        return lax.rem(index + my_group, groups)

    def tile_copy(index):
        place = group_at(index // per_group) * per_group + lax.rem(index, per_group)
        return pltpu.make_async_copy(
            table_hbm.at[place], table_buf.at[index], table_sem.at[index]
        )

    inputs = [
        pltpu.make_async_copy(source, target, in_sem.at[place])
        for place, (source, target) in enumerate(
            [
                (pairs_hbm, pairs_ref),
                (owners_hbm, owners_ref),
                (mask_hbm, mask_ref),
                (strain_hbm, strain_ref),
            ]
        )
    ]
    inputs[3].start()
    tile_copy(0).start()
    for copy in inputs[:3]:
        copy.start()
    for index in range(1, min(AHEAD, tiles)):
        tile_copy(index).start()
    barrier = pltpu.get_barrier_semaphore()

    def greet(step):
        column = lax.rem(mine + step, columns)
        for other in range(groups):
            group = group_at(other)
            if other == 0:

                @pl.when(step > 0)
                def _():
                    pl.semaphore_signal(
                        barrier, inc=1, device_id=(group, column), device_id_type=MESH
                    )

            else:
                pl.semaphore_signal(
                    barrier, inc=1, device_id=(group, column), device_id_type=MESH
                )

    loop(0, columns, greet)
    for copy in inputs:
        copy.wait()
    list_buf[...] = list_row(groups, entries, pairs_ref, owners_ref)

    def compute_tile(index):
        @pl.when(index + AHEAD < tiles)
        def _():
            tile_copy(index + AHEAD).start()

        tile_copy(index).wait()
        spectrum = lax.dot_general(
            table_buf[index],
            strain_ref[...],
            (((1,), (1,)), ((), ())),
            preferred_element_type=jnp.float32,
        )
        lanes = spectrum.shape[1]
        parts = spectrum.reshape(phases, columns, 2, UNIT, lanes)
        power = parts[:, :, 0] * parts[:, :, 0] + parts[:, :, 1] * parts[:, :, 1]
        bands = phases * columns * UNIT // SUB
        power = power.reshape(phases, bands, columns // bands, UNIT, lanes)
        power = jnp.sum(jnp.sum(power, axis=2), axis=0)
        band_power = jnp.sum(power, axis=1, keepdims=True) / SUB
        usable = jnp.concatenate([mask_ref[w : w + 1, :] for w in range(windows)], axis=1)
        gain = usable.astype(jnp.float32).reshape(1, 1, lanes) / jnp.sqrt(band_power + 1e-06)
        gain = gain.reshape(1, bands, 1, 1, lanes)
        white = parts.reshape(phases, bands, columns // bands, unit_rows, lanes) * gain
        white = white.reshape(phases, columns, unit_rows, lanes).astype(jnp.bfloat16)
        for phase in range(phases):
            wave, place = divmod(phase * per_group, wave_subs)
            place = (place + lax.rem(index, per_group)) * unit_rows
            at = pl.ds(pl.multiple_of(place, unit_rows), unit_rows)
            white_buf[index // per_group, wave, :, at, :] = white[phase]

    def white_copy(wave, index, column):
        return pltpu.make_async_remote_copy(
            src_ref=white_buf.at[index, wave, column],
            dst_ref=rows_bufs[wave].at[me],
            send_sem=wsend_sem.at[wave],
            recv_sem=wrecv_sem.at[wave],
            device_id=(group_at(index), column),
            device_id_type=MESH,
        )

    def white_own(wave):
        return pltpu.make_async_copy(
            white_buf.at[0, wave, mine], rows_bufs[wave].at[me], wown_sem.at[wave]
        )

    def send_white(wave, index):
        def send(step):
            white_copy(wave, index, lax.rem(mine + step, columns)).start()

        loop(1, columns, send)

        @pl.when(index == 0)
        def _():
            white_own(wave).start()

        @pl.when(index > 0)
        def _():
            send(0)

    def list_copy(step):
        return pltpu.make_async_remote_copy(
            src_ref=list_buf,
            dst_ref=lists_buf.at[mine],
            send_sem=lsend_sem.at[step],
            recv_sem=lrecv_sem.at[step],
            device_id=(my_group, lax.rem(mine + step, columns)),
            device_id_type=MESH,
        )

    own_list = pltpu.make_async_copy(list_buf, lists_buf.at[mine], own_sem.at[0])

    def send_piece(tile):
        at = pl.ds(pl.multiple_of(tile * unit_rows, unit_rows), unit_rows)

        def send(step):
            pltpu.make_async_remote_copy(
                src_ref=white_buf.at[0, 0, lax.rem(mine + step, columns), at],
                dst_ref=rows_bufs[0].at[me, at],
                send_sem=wsend_sem.at[0],
                recv_sem=wrecv_sem.at[0],
                device_id=(my_group, lax.rem(mine + step, columns)),
                device_id_type=MESH,
            ).start()

        loop(1, columns, send)

    def compute_and_send(index):
        def compute_part(tile):
            compute_tile(index * per_group + tile)

            @pl.when(index == 0)
            def _():
                @pl.when(tile == 0)
                def _():
                    pl.semaphore_wait(barrier, devices - 1)

                send_piece(tile)

                @pl.when(tile == 0)
                def _():
                    loop(1, columns, lambda step: list_copy(step).start())
                    own_list.start()

        loop(0, per_group, compute_part)

        @pl.when(index == 0)
        def _():
            white_own(0).start()

        @pl.when(index > 0)
        def _():
            send_white(0, index)

    loop(0, groups, compute_and_send)
    for wave in range(1, waves):
        loop(0, groups, functools.partial(send_white, wave))
    if phases > 1:
        inverse_copies = [
            pltpu.make_async_copy(inverse_hbm.at[place], target, inverse_sem.at[place])
            for place, target in enumerate([inverse_buf, later_ref])
        ]
        for copy in inverse_copies:
            copy.start()
    own_list.wait()
    loop(1, columns, lambda step: list_copy(step).wait())
    to_smem = pltpu.make_async_copy(lists_buf, lists_smem, own_sem.at[1])
    to_smem.start()
    to_smem.wait()

    def cross(sub, first, second):
        rows_ref = rows_bufs[sub // wave_subs]
        unit = pl.ds(sub % wave_subs * unit_rows, unit_rows)
        real = jnp.zeros((UNIT, BLK), jnp.float32)
        imag = jnp.zeros((UNIT, BLK), jnp.float32)
        for group in range(groups):
            a = rows_ref[group * columns + first, unit].astype(jnp.float32)
            b = rows_ref[group * columns + second, unit].astype(jnp.float32)
            for window in range(windows):
                lanes = slice(window * BLK, (window + 1) * BLK)
                a_real, a_imag = a[:UNIT, lanes], a[UNIT:, lanes]
                b_real, b_imag = b[:UNIT, lanes], b[UNIT:, lanes]
                real += a_real * b_real + a_imag * b_imag
                imag += a_real * b_imag - a_imag * b_real
        return jnp.concatenate([real, imag], axis=0) * scale

    def cross_entries(sub, column, out_ref):
        for entry in range(entries):
            first = lists_smem[column, 0, 2 * entry]
            second = lists_smem[column, 0, 2 * entry + 1]
            out_ref[entry] = cross(sub, first, second).astype(jnp.bfloat16)

    def slot_lane(slot, place):
        return 2 * entries + 4 * slot + place

    def cross_slots(sub, column):
        for group in range(groups):
            for rank in range(CAP):
                slot = group * CAP + rank
                first = lists_smem[column, 0, slot_lane(slot, 0)]
                second = lists_smem[column, 0, slot_lane(slot, 1)]
                used = lists_smem[column, 0, slot_lane(slot, 2)].astype(jnp.float32)
                block = cross(sub, first, second) * used
                slot_buf[group, column, rank] = block.astype(jnp.bfloat16)

    def swap_copy(sub, step):
        return pltpu.make_async_remote_copy(
            src_ref=swap_bufs[sub].at[step - 1],
            dst_ref=entry_bufs[sub][step],
            send_sem=hsend_sem.at[sub, step],
            recv_sem=hrecv_sem.at[sub, step],
            device_id=(my_group, lax.rem(mine + step, columns)),
            device_id_type=MESH,
        )

    def forward_copy(sub, other, source):
        return pltpu.make_async_remote_copy(
            src_ref=forward_bufs[sub].at[other - 1, source],
            dst_ref=stack_bufs[sub].at[:, my_group * columns + source],
            send_sem=fsend_sem.at[sub],
            recv_sem=frecv_sem.at[sub, my_group],
            device_id=(group_at(other), mine),
            device_id_type=MESH,
        )

    def slot_copy(group, column):
        return pltpu.make_async_remote_copy(
            src_ref=slot_buf.at[group, column],
            dst_ref=stack_bufs[hops].at[:, me],
            send_sem=ssend_sem.at[0],
            recv_sem=srecv_sem.at[0],
            device_id=(group, column),
            device_id_type=MESH,
        )

    slot_own = pltpu.make_async_copy(
        slot_buf.at[my_group, mine], stack_bufs[hops].at[:, me], own_sem.at[2]
    )

    def arrived(ref, sem):
        return pltpu.make_async_remote_copy(
            src_ref=ref,
            dst_ref=ref,
            send_sem=sem,
            recv_sem=sem,
            device_id=(lax.rem(my_group + 1, groups), mine),
            device_id_type=MESH,
        )

    def forward(sub, step):
        source = lax.rem(mine - step + columns, columns)
        if step > 0:
            swap_copy(sub, step).wait_recv()
        for other in range(groups):
            for rank in range(CAP):
                slot = group_at(other) * CAP + rank
                used = lists_smem[mine, 0, slot_lane(slot, 2)].astype(jnp.float32)
                entry = lists_smem[mine, 0, slot_lane(slot, 3)]
                block = (entry_bufs[sub][step][entry].astype(jnp.float32) * used).astype(jnp.bfloat16)
                if other == 0:
                    stack_bufs[sub][rank, my_group * columns + source] = block
                else:
                    forward_bufs[sub][other - 1, source, rank] = block
            if other > 0:
                forward_copy(sub, other, source).start()

    def cross_sub(sub):
        if sub % wave_subs == 0:
            wave = sub // wave_subs
            white_own(wave).wait()
            arrived(rows_bufs[wave].at[pl.ds(0, devices - 1)], wrecv_sem.at[wave]).wait_recv()
        if sub < hops:

            def entries_step(step):
                cross_entries(sub, lax.rem(mine + step, columns), swap_bufs[sub].at[step - 1])
                for place in range(1, columns):

                    @pl.when(step == place)
                    def _():
                        swap_copy(sub, place).start()

            loop(1, columns, entries_step)
            cross_entries(sub, mine, entry_bufs[sub][0])
        else:

            def slots_step(step):
                column = lax.rem(mine + step, columns)
                cross_slots(sub, column)
                for other in range(groups):
                    group = group_at(other)
                    if other > 0:
                        slot_copy(group, column).start()
                    else:

                        @pl.when(step < columns)
                        def _():
                            slot_copy(group, column).start()

                        @pl.when(step == columns)
                        def _():
                            slot_own.start()

            loop(1, columns + 1, slots_step)

    def wait_stack(sub):
        def wait(other):
            group = group_at(other)
            part = stack_bufs[sub].at[:, pl.ds(group * columns, columns)]
            arrived(part, frecv_sem.at[sub, group]).wait_recv()

        loop(1, groups, wait)

    for sub in range(subs):
        cross_sub(sub)
        for step in range(columns if 0 < sub else 0):
            forward(sub - 1, step)
    for sub in range(last):
        wait_stack(sub)
    if last > 0:
        for copy in inverse_copies:
            copy.wait()
        transposed(stack_bufs[:last], left_buf)

        def odd_lags(tile):
            at = pl.ds(pl.multiple_of(tile * LAGS, LAGS), LAGS)
            odd_ref[:, at] = jnp.dot(
                left_buf[...], inverse_buf[:, at], preferred_element_type=jnp.float32
            )

        loop(0, NFFT // 2 // LAGS, odd_lags)
    for wave in range(waves):
        arrived(rows_bufs[wave].at[pl.ds(0, devices - 1)], wsend_sem.at[wave]).wait_send()
    for sub in range(hops):
        for step in range(1, columns):
            swap_copy(sub, step).wait_send()
        arrived(forward_bufs[sub], fsend_sem.at[sub]).wait_send()
    for sub in range(last, hops):
        wait_stack(sub)
    others = stack_bufs[hops].at[:, pl.ds(0, devices - 1)]
    arrived(others, ssend_sem.at[0]).wait_send()
    slot_own.wait()
    arrived(others, srecv_sem.at[0]).wait_recv()


def lags_kernel(*refs):
    stack_refs = refs[:-6]
    odd_ref, inverse_ref, out_hbm, left_buf, out_buf, out_sem = refs[-6:]
    transposed(stack_refs, left_buf)
    count = NFFT // 2 // LAGS

    def copies(tile):
        for side in range(2):
            at = pl.ds(side * (NFFT // 2) + tile * LAGS, LAGS)
            yield pltpu.make_async_copy(
                out_buf.at[:, at], out_hbm.at[:, at], out_sem.at[side, tile]
            )

    for tile in range(count):
        at = slice(tile * LAGS, (tile + 1) * LAGS)
        upper = slice(NFFT // 2 + tile * LAGS, NFFT // 2 + (tile + 1) * LAGS)
        even = jnp.dot(left_buf[...], inverse_ref[:, at], preferred_element_type=jnp.float32)
        odd = odd_ref[:, at]
        out_buf[:, at] = even - odd
        out_buf[:, upper] = even + odd
        for copy in copies(tile):
            copy.start()
    for tile in range(count):
        for copy in copies(tile):
            copy.wait()


def local(strain, valid_mask, pair_list, owner_group):
    windows, channels = valid_mask.shape
    groups = lax.axis_size("grp")
    columns = lax.axis_size("ch")
    devices = groups * columns
    entries = owner_group.shape[1]
    phases = phases_of(devices)
    rows = 2 * NB // devices // phases
    lanes = windows * channels
    tiles = NB // (columns * UNIT * phases)
    tile_rows = 2 * NB // tiles
    scale = 1.0 / math.sqrt(NB * windows * groups)

    vmem = pl.BlockSpec(memory_space=pltpu.VMEM)
    anywhere = pl.BlockSpec(memory_space=pltpu.HBM)
    dma = pltpu.SemaphoreType.DMA
    bf16 = jnp.bfloat16
    depth = devices * rows
    per_group = tiles // groups
    subs = phases * per_group
    hops = subs - 1
    waves = min(WAVES, phases)
    last = subs - per_group if phases > 1 else 0
    unit_rows = 2 * UNIT
    stack_shape = (CAP, devices, unit_rows, BLK)
    outs = [jax.ShapeDtypeStruct(stack_shape, bf16) for _ in range(subs - last)]
    if phases > 1:
        outs.append(jax.ShapeDtypeStruct((CAP * BLK, NFFT // 2), jnp.float32))
        outs.append(jax.ShapeDtypeStruct((NB, NFFT // 2), bf16))
    inverse = inverse_rows(groups, columns)
    first_shape = inverse.shape[1:] if phases > 1 else (16, LANES)
    stacks = pl.pallas_call(
        functools.partial(correlate_kernel, groups, columns, phases, entries, windows, scale),
        out_shape=outs,
        in_specs=[anywhere] * 6,
        out_specs=[vmem] * len(outs),
        scratch_shapes=[
            pltpu.SMEM((1, 2, entries), jnp.int32),
            pltpu.SMEM((1, entries), jnp.int32),
            pltpu.VMEM((windows, channels), jnp.int32),
            pltpu.VMEM((lanes, NFFT), bf16),
            pltpu.VMEM(first_shape, bf16),
            pltpu.VMEM((CAP * BLK, depth), bf16),
            pltpu.VMEM((tiles, tile_rows, NFFT), bf16),
            pltpu.VMEM((groups, waves, columns, subs // waves * unit_rows, lanes), bf16),
            pltpu.VMEM((8, LANES), jnp.int32),
            pltpu.VMEM((columns, 8, LANES), jnp.int32),
            pltpu.SMEM((columns, 8, LANES), jnp.int32),
            pltpu.VMEM((groups, columns, CAP, unit_rows, BLK), bf16),
        ]
        + [
            pltpu.VMEM((devices, subs // waves * unit_rows, lanes), bf16)
            for _ in range(waves)
        ]
        + [pltpu.VMEM((columns - 1, entries, unit_rows, BLK), bf16) for _ in range(hops)]
        + [pltpu.VMEM((groups - 1, columns, CAP, unit_rows, BLK), bf16) for _ in range(hops)]
        + [pltpu.VMEM((entries, unit_rows, BLK), bf16) for _ in range(hops * columns)]
        + [pltpu.VMEM(stack_shape, bf16) for _ in range(last)]
        + [dma((4,)), dma((2,)), dma((tiles,)), dma((3,)), dma((columns,)), dma((columns,))]
        + [dma((waves,)), dma((waves,)), dma((waves,))]
        + [dma((max(1, hops), columns)), dma((max(1, hops), columns))]
        + [dma((max(1, hops),)), dma((max(1, hops), groups)), dma((1,)), dma((1,))],
        compiler_params=pltpu.CompilerParams(
            collective_id=0, has_side_effects=True, vmem_limit_bytes=44 * 1024 * 1024
        ),
    )(
        *[
            pltpu.with_memory_space_constraint(operand, pltpu.HBM)
            for operand in (
                pair_list.transpose(0, 2, 1),
                owner_group,
                valid_mask,
                strain.reshape(lanes, NFFT),
                jnp.asarray(forward_rows(groups, columns)).reshape(tiles, tile_rows, NFFT),
                jnp.asarray(inverse if phases > 1 else np.zeros(first_shape, bf16)),
            )
        ]
    )
    if phases > 1:
        stacked = pl.pallas_call(
            lags_kernel,
            out_shape=jax.ShapeDtypeStruct((CAP * BLK, NFFT), jnp.float32),
            in_specs=[vmem] * len(outs),
            out_specs=anywhere,
            scratch_shapes=[
                pltpu.VMEM((CAP * BLK, depth), bf16),
                pltpu.VMEM((CAP * BLK, NFFT), jnp.float32),
                dma((2, NFFT // 2 // LAGS)),
            ],
            compiler_params=pltpu.CompilerParams(vmem_limit_bytes=44 * 1024 * 1024),
        )(*stacks)
    else:
        stacked = jnp.einsum(
            "skr,kt->srt",
            stacks[0].reshape(CAP, depth, BLK),
            jnp.asarray(inverse[0]),
            preferred_element_type=jnp.float32,
        )
    return stacked.reshape(1, 1, CAP, BLK, NFFT)


def solution(mesh):
    placed = (P("grp", "ch", None), P("grp", "ch"), P("ch", None, None), P("ch", None))
    return jax.shard_map(
        local,
        mesh=mesh,
        in_specs=placed,
        out_specs=P("grp", "ch", None, None, None),
        check_vma=False,
    )
```

```python
import functools
import math

import jax
import jax.numpy as jnp
import numpy as np
from jax import lax
from jax.experimental import pallas as pl
from jax.experimental.pallas import tpu as pltpu
from jax.sharding import PartitionSpec as P

NFFT = 4096
NB = 1024
SUB = 64
BLK = 128
CAP = 2
LANES = 128
UNIT = 8
LAGS = 512
AHEAD = 2
WAVES = 2
MESH = pl.DeviceIdType.MESH


def phases_of(devices):
    return 2 if NB // devices % (2 * UNIT) == 0 else 1


def bin_numbers(groups, columns):
    phases = phases_of(groups * columns)
    tile_bins = columns * UNIT * phases
    bins = 1 + np.arange(NB, dtype=np.int64)
    bins = bins.reshape(groups, NB // tile_bins // groups, columns, UNIT, phases)
    return bins.transpose(0, 1, 4, 2, 3)


def table_rows(bins, samples, taper):
    angles = np.mod(bins[..., None, :, None] * samples, NFFT) * (2.0 * math.pi / NFFT)
    rows = np.concatenate([np.cos(angles), -np.sin(angles)], axis=-3) * taper
    return rows.reshape(2 * bins.size, len(samples)).astype(jnp.bfloat16)


@functools.lru_cache(maxsize=None)
def forward_rows(groups, columns):
    samples = np.arange(NFFT, dtype=np.int64)
    taper = 0.5 - 0.5 * np.cos(samples * (2.0 * math.pi / NFFT))
    return table_rows(bin_numbers(groups, columns), samples, taper)


@functools.lru_cache(maxsize=None)
def inverse_rows(groups, columns):
    phases = phases_of(groups * columns)
    bins = bin_numbers(groups, columns).transpose(2, 1, 0, 3, 4)
    samples = np.arange(NFFT, dtype=np.int64) - NFFT // 2
    if phases > 1:
        samples = samples[NFFT // 2 :]
    rows = table_rows(bins, samples, np.ones(len(samples)))
    return rows.reshape(phases, 2 * NB // phases, len(samples))


def loop(low, high, body):
    def step_body(step, carry):
        body(step)
        return carry

    lax.fori_loop(low, high, step_body, 0)


def transposed(stack_refs, left_ref):
    for place, stack_ref in enumerate(stack_refs):
        depth = stack_ref.shape[1] * stack_ref.shape[2]
        for rank in range(CAP):
            block = stack_ref[rank].reshape(depth, BLK).astype(jnp.float32)
            rows = slice(rank * BLK, (rank + 1) * BLK)
            left_ref[rows, place * depth : (place + 1) * depth] = block.T.astype(jnp.bfloat16)


def list_row(groups, entries, pairs_ref, owners_ref):
    lane = lax.broadcasted_iota(jnp.int32, (8, LANES), 1)
    row = jnp.zeros((8, LANES), jnp.int32)
    for entry in range(entries):
        owner = owners_ref[0, entry]
        rank = jnp.int32(0)
        for before in range(entry):
            rank += (owners_ref[0, before] == owner).astype(jnp.int32)
        base = 2 * entries + 4 * (owner * CAP + rank)
        for side in range(2):
            block = pairs_ref[0, side, entry]
            row = jnp.where((lane == 2 * entry + side) | (lane == base + side), block, row)
        row = jnp.where(lane == base + 2, 1, row)
        row = jnp.where(lane == base + 3, entry, row)
    return row


def correlate_kernel(
    groups, columns, phases, entries, windows, scale,
    pairs_hbm, owners_hbm, mask_hbm, strain_hbm, table_hbm, inverse_hbm, *rest,
):
    per_group = table_hbm.shape[0] // groups
    subs = phases * per_group
    hops = subs - 1
    last = subs - per_group if phases > 1 else 0
    rest = list(rest)
    take = lambda count: [rest.pop(0) for _ in range(count)]
    out_stacks = take(subs - last)
    odd_ref, later_ref = take(2) if phases > 1 else (None, None)
    pairs_ref, owners_ref, mask_ref, strain_ref, inverse_buf, left_buf = take(6)
    table_buf, white_buf, list_buf, lists_buf, lists_smem, slot_buf = take(6)
    waves = white_buf.shape[1]
    wave_subs = subs // waves
    rows_bufs, swap_bufs, forward_bufs = take(waves), take(hops), take(hops)
    entry_bufs = [take(columns) for _ in range(hops)]
    stack_bufs = take(last) + out_stacks
    in_sem, inverse_sem, table_sem, own_sem, lsend_sem, lrecv_sem = take(6)
    wown_sem, wsend_sem, wrecv_sem, hsend_sem, hrecv_sem, fsend_sem, frecv_sem = take(7)
    ssend_sem, srecv_sem = take(2)
    devices = groups * columns
    my_group = lax.axis_index("grp")
    mine = lax.axis_index("ch")
    me = my_group * columns + mine
    tiles = table_buf.shape[0]
    unit_rows = 2 * UNIT

    def group_at(index):
        return lax.rem(index + my_group, groups)

    def tile_copy(index):
        place = group_at(index // per_group) * per_group + lax.rem(index, per_group)
        return pltpu.make_async_copy(
            table_hbm.at[place], table_buf.at[index], table_sem.at[index]
        )

    inputs = [
        pltpu.make_async_copy(source, target, in_sem.at[place])
        for place, (source, target) in enumerate(
            [
                (pairs_hbm, pairs_ref),
                (owners_hbm, owners_ref),
                (mask_hbm, mask_ref),
                (strain_hbm, strain_ref),
            ]
        )
    ]
    inputs[3].start()
    tile_copy(0).start()
    for copy in inputs[:3]:
        copy.start()
    for index in range(1, min(AHEAD, tiles)):
        tile_copy(index).start()
    barrier = pltpu.get_barrier_semaphore()

    def greet(step):
        column = lax.rem(mine + step, columns)
        for other in range(groups):
            group = group_at(other)
            if other == 0:

                @pl.when(step > 0)
                def _():
                    pl.semaphore_signal(
                        barrier, inc=1, device_id=(group, column), device_id_type=MESH
                    )

            else:
                pl.semaphore_signal(
                    barrier, inc=1, device_id=(group, column), device_id_type=MESH
                )

    loop(0, columns, greet)
    for copy in inputs:
        copy.wait()
    list_buf[...] = list_row(groups, entries, pairs_ref, owners_ref)

    def compute_tile(index):
        @pl.when(index + AHEAD < tiles)
        def _():
            tile_copy(index + AHEAD).start()

        tile_copy(index).wait()
        spectrum = lax.dot_general(
            table_buf[index],
            strain_ref[...],
            (((1,), (1,)), ((), ())),
            preferred_element_type=jnp.float32,
        )
        lanes = spectrum.shape[1]
        parts = spectrum.reshape(phases, columns, 2, UNIT, lanes)
        power = parts[:, :, 0] * parts[:, :, 0] + parts[:, :, 1] * parts[:, :, 1]
        bands = phases * columns * UNIT // SUB
        power = power.reshape(phases, bands, columns // bands, UNIT, lanes)
        power = jnp.sum(jnp.sum(power, axis=2), axis=0)
        band_power = jnp.sum(power, axis=1, keepdims=True) / SUB
        usable = jnp.concatenate([mask_ref[w : w + 1, :] for w in range(windows)], axis=1)
        gain = usable.astype(jnp.float32).reshape(1, 1, lanes) / jnp.sqrt(band_power + 1e-06)
        gain = gain.reshape(1, bands, 1, 1, lanes)
        white = parts.reshape(phases, bands, columns // bands, unit_rows, lanes) * gain
        white = white.reshape(phases, columns, unit_rows, lanes).astype(jnp.bfloat16)
        for phase in range(phases):
            wave, place = divmod(phase * per_group, wave_subs)
            place = (place + lax.rem(index, per_group)) * unit_rows
            at = pl.ds(pl.multiple_of(place, unit_rows), unit_rows)
            white_buf[index // per_group, wave, :, at, :] = white[phase]

    def white_copy(wave, index, column):
        return pltpu.make_async_remote_copy(
            src_ref=white_buf.at[index, wave, column],
            dst_ref=rows_bufs[wave].at[me],
            send_sem=wsend_sem.at[wave],
            recv_sem=wrecv_sem.at[wave],
            device_id=(group_at(index), column),
            device_id_type=MESH,
        )

    def white_own(wave):
        return pltpu.make_async_copy(
            white_buf.at[0, wave, mine], rows_bufs[wave].at[me], wown_sem.at[wave]
        )

    def send_white(wave, index):
        def send(step):
            white_copy(wave, index, lax.rem(mine + step, columns)).start()

        loop(1, columns, send)

        @pl.when(index == 0)
        def _():
            white_own(wave).start()

        @pl.when(index > 0)
        def _():
            send(0)

    def list_copy(step):
        return pltpu.make_async_remote_copy(
            src_ref=list_buf,
            dst_ref=lists_buf.at[mine],
            send_sem=lsend_sem.at[step],
            recv_sem=lrecv_sem.at[step],
            device_id=(my_group, lax.rem(mine + step, columns)),
            device_id_type=MESH,
        )

    own_list = pltpu.make_async_copy(list_buf, lists_buf.at[mine], own_sem.at[0])

    def send_piece(tile):
        at = pl.ds(pl.multiple_of(tile * unit_rows, unit_rows), unit_rows)

        def send(step):
            pltpu.make_async_remote_copy(
                src_ref=white_buf.at[0, 0, lax.rem(mine + step, columns), at],
                dst_ref=rows_bufs[0].at[me, at],
                send_sem=wsend_sem.at[0],
                recv_sem=wrecv_sem.at[0],
                device_id=(my_group, lax.rem(mine + step, columns)),
                device_id_type=MESH,
            ).start()

        loop(1, columns, send)

    def compute_and_send(index):
        def compute_part(tile):
            compute_tile(index * per_group + tile)

            @pl.when(index == 0)
            def _():
                @pl.when(tile == 0)
                def _():
                    pl.semaphore_wait(barrier, devices - 1)

                send_piece(tile)

                @pl.when(tile == 0)
                def _():
                    loop(1, columns, lambda step: list_copy(step).start())
                    own_list.start()

        loop(0, per_group, compute_part)

        @pl.when(index == 0)
        def _():
            white_own(0).start()

        @pl.when(index > 0)
        def _():
            send_white(0, index)

    loop(0, groups, compute_and_send)
    for wave in range(1, waves):
        loop(0, groups, functools.partial(send_white, wave))
    if phases > 1:
        inverse_copies = [
            pltpu.make_async_copy(inverse_hbm.at[place], target, inverse_sem.at[place])
            for place, target in enumerate([inverse_buf, later_ref])
        ]
        for copy in inverse_copies:
            copy.start()
    own_list.wait()
    loop(1, columns, lambda step: list_copy(step).wait())
    to_smem = pltpu.make_async_copy(lists_buf, lists_smem, own_sem.at[1])
    to_smem.start()
    to_smem.wait()

    def cross(sub, first, second):
        rows_ref = rows_bufs[sub // wave_subs]
        unit = pl.ds(sub % wave_subs * unit_rows, unit_rows)
        real = jnp.zeros((UNIT, BLK), jnp.float32)
        imag = jnp.zeros((UNIT, BLK), jnp.float32)
        for group in range(groups):
            a = rows_ref[group * columns + first, unit].astype(jnp.float32)
            b = rows_ref[group * columns + second, unit].astype(jnp.float32)
            for window in range(windows):
                lanes = slice(window * BLK, (window + 1) * BLK)
                a_real, a_imag = a[:UNIT, lanes], a[UNIT:, lanes]
                b_real, b_imag = b[:UNIT, lanes], b[UNIT:, lanes]
                real += a_real * b_real + a_imag * b_imag
                imag += a_real * b_imag - a_imag * b_real
        return jnp.concatenate([real, imag], axis=0) * scale

    def cross_entries(sub, column, out_ref):
        for entry in range(entries):
            first = lists_smem[column, 0, 2 * entry]
            second = lists_smem[column, 0, 2 * entry + 1]
            out_ref[entry] = cross(sub, first, second).astype(jnp.bfloat16)

    def slot_lane(slot, place):
        return 2 * entries + 4 * slot + place

    def cross_slots(sub, column):
        for group in range(groups):
            for rank in range(CAP):
                slot = group * CAP + rank
                first = lists_smem[column, 0, slot_lane(slot, 0)]
                second = lists_smem[column, 0, slot_lane(slot, 1)]
                used = lists_smem[column, 0, slot_lane(slot, 2)].astype(jnp.float32)
                block = cross(sub, first, second) * used
                slot_buf[group, column, rank] = block.astype(jnp.bfloat16)

    def swap_copy(sub, step):
        return pltpu.make_async_remote_copy(
            src_ref=swap_bufs[sub].at[step - 1],
            dst_ref=entry_bufs[sub][step],
            send_sem=hsend_sem.at[sub, step],
            recv_sem=hrecv_sem.at[sub, step],
            device_id=(my_group, lax.rem(mine + step, columns)),
            device_id_type=MESH,
        )

    def forward_copy(sub, other, source):
        return pltpu.make_async_remote_copy(
            src_ref=forward_bufs[sub].at[other - 1, source],
            dst_ref=stack_bufs[sub].at[:, my_group * columns + source],
            send_sem=fsend_sem.at[sub],
            recv_sem=frecv_sem.at[sub, my_group],
            device_id=(group_at(other), mine),
            device_id_type=MESH,
        )

    def slot_copy(group, column):
        return pltpu.make_async_remote_copy(
            src_ref=slot_buf.at[group, column],
            dst_ref=stack_bufs[hops].at[:, me],
            send_sem=ssend_sem.at[0],
            recv_sem=srecv_sem.at[0],
            device_id=(group, column),
            device_id_type=MESH,
        )

    slot_own = pltpu.make_async_copy(
        slot_buf.at[my_group, mine], stack_bufs[hops].at[:, me], own_sem.at[2]
    )

    def arrived(ref, sem):
        return pltpu.make_async_remote_copy(
            src_ref=ref,
            dst_ref=ref,
            send_sem=sem,
            recv_sem=sem,
            device_id=(lax.rem(my_group + 1, groups), mine),
            device_id_type=MESH,
        )

    def forward(sub, step):
        source = lax.rem(mine - step + columns, columns)
        if step > 0:
            swap_copy(sub, step).wait_recv()
        for other in range(groups):
            for rank in range(CAP):
                slot = group_at(other) * CAP + rank
                used = lists_smem[mine, 0, slot_lane(slot, 2)].astype(jnp.float32)
                entry = lists_smem[mine, 0, slot_lane(slot, 3)]
                block = (entry_bufs[sub][step][entry].astype(jnp.float32) * used).astype(jnp.bfloat16)
                if other == 0:
                    stack_bufs[sub][rank, my_group * columns + source] = block
                else:
                    forward_bufs[sub][other - 1, source, rank] = block
            if other > 0:
                forward_copy(sub, other, source).start()

    def cross_sub(sub):
        if sub % wave_subs == 0:
            wave = sub // wave_subs
            white_own(wave).wait()
            arrived(rows_bufs[wave].at[pl.ds(0, devices - 1)], wrecv_sem.at[wave]).wait_recv()
        if sub < hops:

            def entries_step(step):
                cross_entries(sub, lax.rem(mine + step, columns), swap_bufs[sub].at[step - 1])
                for place in range(1, columns):

                    @pl.when(step == place)
                    def _():
                        swap_copy(sub, place).start()

            loop(1, columns, entries_step)
            cross_entries(sub, mine, entry_bufs[sub][0])
        else:

            def slots_step(step):
                column = lax.rem(mine + step, columns)
                cross_slots(sub, column)
                for other in range(groups):
                    group = group_at(other)
                    if other > 0:
                        slot_copy(group, column).start()
                    else:

                        @pl.when(step < columns)
                        def _():
                            slot_copy(group, column).start()

                        @pl.when(step == columns)
                        def _():
                            slot_own.start()

            loop(1, columns + 1, slots_step)

    def wait_stack(sub):
        def wait(other):
            group = group_at(other)
            part = stack_bufs[sub].at[:, pl.ds(group * columns, columns)]
            arrived(part, frecv_sem.at[sub, group]).wait_recv()

        loop(1, groups, wait)

    for sub in range(subs):
        cross_sub(sub)
        for step in range(columns if 0 < sub else 0):
            forward(sub - 1, step)
    for sub in range(last):
        wait_stack(sub)
    if last > 0:
        for copy in inverse_copies:
            copy.wait()
        transposed(stack_bufs[:last], left_buf)

        def odd_lags(tile):
            at = pl.ds(pl.multiple_of(tile * LAGS, LAGS), LAGS)
            odd_ref[:, at] = jnp.dot(
                left_buf[...], inverse_buf[:, at], preferred_element_type=jnp.float32
            )

        loop(0, NFFT // 2 // LAGS, odd_lags)
    for wave in range(waves):
        arrived(rows_bufs[wave].at[pl.ds(0, devices - 1)], wsend_sem.at[wave]).wait_send()
    for sub in range(hops):
        for step in range(1, columns):
            swap_copy(sub, step).wait_send()
        arrived(forward_bufs[sub], fsend_sem.at[sub]).wait_send()
    for sub in range(last, hops):
        wait_stack(sub)
    others = stack_bufs[hops].at[:, pl.ds(0, devices - 1)]
    arrived(others, ssend_sem.at[0]).wait_send()
    slot_own.wait()
    arrived(others, srecv_sem.at[0]).wait_recv()


def lags_kernel(*refs):
    stack_refs = refs[:-6]
    odd_ref, inverse_ref, out_hbm, left_buf, out_buf, out_sem = refs[-6:]
    transposed(stack_refs, left_buf)
    count = NFFT // 2 // LAGS

    def copies(tile):
        for side in range(2):
            at = pl.ds(side * (NFFT // 2) + tile * LAGS, LAGS)
            yield pltpu.make_async_copy(
                out_buf.at[:, at], out_hbm.at[:, at], out_sem.at[side, tile]
            )

    for tile in range(count):
        at = slice(tile * LAGS, (tile + 1) * LAGS)
        upper = slice(NFFT // 2 + tile * LAGS, NFFT // 2 + (tile + 1) * LAGS)
        even = jnp.dot(left_buf[...], inverse_ref[:, at], preferred_element_type=jnp.float32)
        odd = odd_ref[:, at]
        out_buf[:, at] = even - odd
        out_buf[:, upper] = even + odd
        for copy in copies(tile):
            copy.start()
    for tile in range(count):
        for copy in copies(tile):
            copy.wait()


def local(strain, valid_mask, pair_list, owner_group):
    windows, channels = valid_mask.shape
    groups = lax.axis_size("grp")
    columns = lax.axis_size("ch")
    devices = groups * columns
    entries = owner_group.shape[1]
    phases = phases_of(devices)
    rows = 2 * NB // devices // phases
    lanes = windows * channels
    tiles = NB // (columns * UNIT * phases)
    tile_rows = 2 * NB // tiles
    scale = 1.0 / math.sqrt(NB * windows * groups)

    vmem = pl.BlockSpec(memory_space=pltpu.VMEM)
    anywhere = pl.BlockSpec(memory_space=pltpu.HBM)
    dma = pltpu.SemaphoreType.DMA
    bf16 = jnp.bfloat16
    depth = devices * rows
    per_group = tiles // groups
    subs = phases * per_group
    hops = subs - 1
    waves = min(WAVES, phases)
    last = subs - per_group if phases > 1 else 0
    unit_rows = 2 * UNIT
    stack_shape = (CAP, devices, unit_rows, BLK)
    outs = [jax.ShapeDtypeStruct(stack_shape, bf16) for _ in range(subs - last)]
    if phases > 1:
        outs.append(jax.ShapeDtypeStruct((CAP * BLK, NFFT // 2), jnp.float32))
        outs.append(jax.ShapeDtypeStruct((NB, NFFT // 2), bf16))
    inverse = inverse_rows(groups, columns)
    first_shape = inverse.shape[1:] if phases > 1 else (16, LANES)
    stacks = pl.pallas_call(
        functools.partial(correlate_kernel, groups, columns, phases, entries, windows, scale),
        out_shape=outs,
        in_specs=[anywhere] * 6,
        out_specs=[vmem] * len(outs),
        scratch_shapes=[
            pltpu.SMEM((1, 2, entries), jnp.int32),
            pltpu.SMEM((1, entries), jnp.int32),
            pltpu.VMEM((windows, channels), jnp.int32),
            pltpu.VMEM((lanes, NFFT), bf16),
            pltpu.VMEM(first_shape, bf16),
            pltpu.VMEM((CAP * BLK, depth), bf16),
            pltpu.VMEM((tiles, tile_rows, NFFT), bf16),
            pltpu.VMEM((groups, waves, columns, subs // waves * unit_rows, lanes), bf16),
            pltpu.VMEM((8, LANES), jnp.int32),
            pltpu.VMEM((columns, 8, LANES), jnp.int32),
            pltpu.SMEM((columns, 8, LANES), jnp.int32),
            pltpu.VMEM((groups, columns, CAP, unit_rows, BLK), bf16),
        ]
        + [
            pltpu.VMEM((devices, subs // waves * unit_rows, lanes), bf16)
            for _ in range(waves)
        ]
        + [pltpu.VMEM((columns - 1, entries, unit_rows, BLK), bf16) for _ in range(hops)]
        + [pltpu.VMEM((groups - 1, columns, CAP, unit_rows, BLK), bf16) for _ in range(hops)]
        + [pltpu.VMEM((entries, unit_rows, BLK), bf16) for _ in range(hops * columns)]
        + [pltpu.VMEM(stack_shape, bf16) for _ in range(last)]
        + [dma((4,)), dma((2,)), dma((tiles,)), dma((3,)), dma((columns,)), dma((columns,))]
        + [dma((waves,)), dma((waves,)), dma((waves,))]
        + [dma((max(1, hops), columns)), dma((max(1, hops), columns))]
        + [dma((max(1, hops),)), dma((max(1, hops), groups)), dma((1,)), dma((1,))],
        compiler_params=pltpu.CompilerParams(
            collective_id=0, has_side_effects=True, vmem_limit_bytes=44 * 1024 * 1024
        ),
    )(
        *[
            pltpu.with_memory_space_constraint(operand, pltpu.HBM)
            for operand in (
                pair_list.transpose(0, 2, 1),
                owner_group,
                valid_mask,
                strain.reshape(lanes, NFFT),
                jnp.asarray(forward_rows(groups, columns)).reshape(tiles, tile_rows, NFFT),
                jnp.asarray(inverse if phases > 1 else np.zeros(first_shape, bf16)),
            )
        ]
    )
    if phases > 1:
        stacked = pl.pallas_call(
            lags_kernel,
            out_shape=jax.ShapeDtypeStruct((CAP * BLK, NFFT), jnp.float32),
            in_specs=[vmem] * len(outs),
            out_specs=anywhere,
            scratch_shapes=[
                pltpu.VMEM((CAP * BLK, depth), bf16),
                pltpu.VMEM((CAP * BLK, NFFT), jnp.float32),
                dma((2, NFFT // 2 // LAGS)),
            ],
            compiler_params=pltpu.CompilerParams(vmem_limit_bytes=44 * 1024 * 1024),
        )(*stacks)
    else:
        stacked = jnp.einsum(
            "skr,kt->srt",
            stacks[0].reshape(CAP, depth, BLK),
            jnp.asarray(inverse[0]),
            preferred_element_type=jnp.float32,
        )
    return stacked.reshape(1, 1, CAP, BLK, NFFT)


def solution(mesh):
    placed = (P("grp", "ch", None), P("grp", "ch"), P("ch", None, None), P("ch", None))
    return jax.shard_map(
        local,
        mesh=mesh,
        in_specs=placed,
        out_specs=P("grp", "ch", None, None, None),
        check_vma=False,
    )
```

```python
import functools
import math

import jax
import jax.numpy as jnp
import numpy as np
from jax import lax
from jax.experimental import pallas as pl
from jax.experimental.pallas import tpu as pltpu
from jax.sharding import PartitionSpec as P

NFFT = 4096
NB = 1024
SUB = 64
BLK = 128
CAP = 2
LANES = 128
UNIT = 8
LAGS = 512
AHEAD = 2
WAVES = 2
MESH = pl.DeviceIdType.MESH


def phases_of(devices):
    return 2 if NB // devices % (2 * UNIT) == 0 else 1


def bin_numbers(groups, columns):
    phases = phases_of(groups * columns)
    tile_bins = columns * UNIT * phases
    bins = 1 + np.arange(NB, dtype=np.int64)
    bins = bins.reshape(groups, NB // tile_bins // groups, columns, UNIT, phases)
    return bins.transpose(0, 1, 4, 2, 3)


def table_rows(bins, samples, taper):
    angles = np.mod(bins[..., None, :, None] * samples, NFFT) * (2.0 * math.pi / NFFT)
    rows = np.concatenate([np.cos(angles), -np.sin(angles)], axis=-3) * taper
    return rows.reshape(2 * bins.size, len(samples)).astype(jnp.bfloat16)


@functools.lru_cache(maxsize=None)
def forward_rows(groups, columns):
    samples = np.arange(NFFT, dtype=np.int64)
    taper = 0.5 - 0.5 * np.cos(samples * (2.0 * math.pi / NFFT))
    return table_rows(bin_numbers(groups, columns), samples, taper)


@functools.lru_cache(maxsize=None)
def inverse_rows(groups, columns):
    phases = phases_of(groups * columns)
    bins = bin_numbers(groups, columns).transpose(2, 1, 0, 3, 4)
    samples = np.arange(NFFT, dtype=np.int64) - NFFT // 2
    if phases > 1:
        samples = samples[NFFT // 2 :]
    rows = table_rows(bins, samples, np.ones(len(samples)))
    return rows.reshape(phases, 2 * NB // phases, len(samples))


def loop(low, high, body):
    def step_body(step, carry):
        body(step)
        return carry

    lax.fori_loop(low, high, step_body, 0)


def transposed(stack_refs, left_ref):
    for place, stack_ref in enumerate(stack_refs):
        depth = stack_ref.shape[1] * stack_ref.shape[2]
        for rank in range(CAP):
            block = stack_ref[rank].reshape(depth, BLK).astype(jnp.float32)
            rows = slice(rank * BLK, (rank + 1) * BLK)
            left_ref[rows, place * depth : (place + 1) * depth] = block.T.astype(jnp.bfloat16)


def list_row(groups, entries, pairs_ref, owners_ref):
    lane = lax.broadcasted_iota(jnp.int32, (8, LANES), 1)
    row = jnp.zeros((8, LANES), jnp.int32)
    for entry in range(entries):
        owner = owners_ref[0, entry]
        rank = jnp.int32(0)
        for before in range(entry):
            rank += (owners_ref[0, before] == owner).astype(jnp.int32)
        base = 2 * entries + 4 * (owner * CAP + rank)
        for side in range(2):
            block = pairs_ref[0, side, entry]
            row = jnp.where((lane == 2 * entry + side) | (lane == base + side), block, row)
        row = jnp.where(lane == base + 2, 1, row)
        row = jnp.where(lane == base + 3, entry, row)
    return row


def correlate_kernel(
    groups, columns, phases, entries, windows, scale,
    pairs_hbm, owners_hbm, mask_hbm, strain_hbm, table_hbm, inverse_hbm, *rest,
):
    per_group = table_hbm.shape[0] // groups
    subs = phases * per_group
    hops = subs - 1
    last = subs - per_group if phases > 1 else 0
    rest = list(rest)
    take = lambda count: [rest.pop(0) for _ in range(count)]
    out_stacks = take(subs - last)
    odd_ref, later_ref = take(2) if phases > 1 else (None, None)
    pairs_ref, owners_ref, mask_ref, strain_ref, inverse_buf, left_buf = take(6)
    table_buf, white_buf, list_buf, lists_buf, lists_smem, slot_buf = take(6)
    waves = white_buf.shape[1]
    wave_subs = subs // waves
    rows_bufs, swap_bufs, forward_bufs = take(waves), take(hops), take(hops)
    entry_bufs = [take(columns) for _ in range(hops)]
    stack_bufs = take(last) + out_stacks
    in_sem, inverse_sem, table_sem, own_sem, lsend_sem, lrecv_sem = take(6)
    wown_sem, wsend_sem, wrecv_sem, hsend_sem, hrecv_sem, fsend_sem, frecv_sem = take(7)
    ssend_sem, srecv_sem = take(2)
    devices = groups * columns
    my_group = lax.axis_index("grp")
    mine = lax.axis_index("ch")
    me = my_group * columns + mine
    tiles = table_buf.shape[0]
    unit_rows = 2 * UNIT

    def group_at(index):
        return lax.rem(index + my_group, groups)

    def tile_copy(index):
        place = group_at(index // per_group) * per_group + lax.rem(index, per_group)
        return pltpu.make_async_copy(
            table_hbm.at[place], table_buf.at[index], table_sem.at[index]
        )

    inputs = [
        pltpu.make_async_copy(source, target, in_sem.at[place])
        for place, (source, target) in enumerate(
            [
                (pairs_hbm, pairs_ref),
                (owners_hbm, owners_ref),
                (mask_hbm, mask_ref),
                (strain_hbm, strain_ref),
            ]
        )
    ]
    inputs[3].start()
    tile_copy(0).start()
    for copy in inputs[:3]:
        copy.start()
    for index in range(1, min(AHEAD, tiles)):
        tile_copy(index).start()
    barrier = pltpu.get_barrier_semaphore()

    def greet(step):
        column = lax.rem(mine + step, columns)
        for other in range(groups):
            group = group_at(other)
            if other == 0:

                @pl.when(step > 0)
                def _():
                    pl.semaphore_signal(
                        barrier, inc=1, device_id=(group, column), device_id_type=MESH
                    )

            else:
                pl.semaphore_signal(
                    barrier, inc=1, device_id=(group, column), device_id_type=MESH
                )

    loop(0, columns, greet)
    for copy in inputs:
        copy.wait()
    list_buf[...] = list_row(groups, entries, pairs_ref, owners_ref)

    def compute_tile(index):
        @pl.when(index + AHEAD < tiles)
        def _():
            tile_copy(index + AHEAD).start()

        tile_copy(index).wait()
        spectrum = lax.dot_general(
            table_buf[index],
            strain_ref[...],
            (((1,), (1,)), ((), ())),
            preferred_element_type=jnp.float32,
        )
        lanes = spectrum.shape[1]
        parts = spectrum.reshape(phases, columns, 2, UNIT, lanes)
        power = parts[:, :, 0] * parts[:, :, 0] + parts[:, :, 1] * parts[:, :, 1]
        bands = phases * columns * UNIT // SUB
        power = power.reshape(phases, bands, columns // bands, UNIT, lanes)
        power = jnp.sum(jnp.sum(power, axis=2), axis=0)
        band_power = jnp.sum(power, axis=1, keepdims=True) / SUB
        usable = jnp.concatenate([mask_ref[w : w + 1, :] for w in range(windows)], axis=1)
        gain = usable.astype(jnp.float32).reshape(1, 1, lanes) / jnp.sqrt(band_power + 1e-06)
        gain = gain.reshape(1, bands, 1, 1, lanes)
        white = parts.reshape(phases, bands, columns // bands, unit_rows, lanes) * gain
        white = white.reshape(phases, columns, unit_rows, lanes).astype(jnp.bfloat16)
        for phase in range(phases):
            wave, place = divmod(phase * per_group, wave_subs)
            place = (place + lax.rem(index, per_group)) * unit_rows
            at = pl.ds(pl.multiple_of(place, unit_rows), unit_rows)
            white_buf[index // per_group, wave, :, at, :] = white[phase]

    def white_copy(wave, index, column):
        return pltpu.make_async_remote_copy(
            src_ref=white_buf.at[index, wave, column],
            dst_ref=rows_bufs[wave].at[me],
            send_sem=wsend_sem.at[wave],
            recv_sem=wrecv_sem.at[wave],
            device_id=(group_at(index), column),
            device_id_type=MESH,
        )

    def white_own(wave):
        return pltpu.make_async_copy(
            white_buf.at[0, wave, mine], rows_bufs[wave].at[me], wown_sem.at[wave]
        )

    def send_white(wave, index):
        def send(step):
            white_copy(wave, index, lax.rem(mine + step, columns)).start()

        loop(1, columns, send)

        @pl.when(index == 0)
        def _():
            white_own(wave).start()

        @pl.when(index > 0)
        def _():
            send(0)

    def list_copy(step):
        return pltpu.make_async_remote_copy(
            src_ref=list_buf,
            dst_ref=lists_buf.at[mine],
            send_sem=lsend_sem.at[step],
            recv_sem=lrecv_sem.at[step],
            device_id=(my_group, lax.rem(mine + step, columns)),
            device_id_type=MESH,
        )

    own_list = pltpu.make_async_copy(list_buf, lists_buf.at[mine], own_sem.at[0])

    def send_piece(tile):
        at = pl.ds(pl.multiple_of(tile * unit_rows, unit_rows), unit_rows)

        def send(step):
            pltpu.make_async_remote_copy(
                src_ref=white_buf.at[0, 0, lax.rem(mine + step, columns), at],
                dst_ref=rows_bufs[0].at[me, at],
                send_sem=wsend_sem.at[0],
                recv_sem=wrecv_sem.at[0],
                device_id=(my_group, lax.rem(mine + step, columns)),
                device_id_type=MESH,
            ).start()

        loop(1, columns, send)

    def compute_and_send(index):
        def compute_part(tile):
            compute_tile(index * per_group + tile)

            @pl.when(index == 0)
            def _():
                @pl.when(tile == 0)
                def _():
                    pl.semaphore_wait(barrier, devices - 1)

                send_piece(tile)

                @pl.when(tile == 0)
                def _():
                    loop(1, columns, lambda step: list_copy(step).start())
                    own_list.start()

        loop(0, per_group, compute_part)

        @pl.when(index == 0)
        def _():
            white_own(0).start()

        @pl.when(index > 0)
        def _():
            send_white(0, index)

    loop(0, groups, compute_and_send)
    for wave in range(1, waves):
        loop(0, groups, functools.partial(send_white, wave))
    if phases > 1:
        inverse_copies = [
            pltpu.make_async_copy(inverse_hbm.at[place], target, inverse_sem.at[place])
            for place, target in enumerate([inverse_buf, later_ref])
        ]
    own_list.wait()
    loop(1, columns, lambda step: list_copy(step).wait())
    to_smem = pltpu.make_async_copy(lists_buf, lists_smem, own_sem.at[1])
    to_smem.start()
    to_smem.wait()

    def cross(sub, first, second):
        rows_ref = rows_bufs[sub // wave_subs]
        unit = pl.ds(sub % wave_subs * unit_rows, unit_rows)
        real = jnp.zeros((UNIT, BLK), jnp.float32)
        imag = jnp.zeros((UNIT, BLK), jnp.float32)
        for group in range(groups):
            a = rows_ref[group * columns + first, unit].astype(jnp.float32)
            b = rows_ref[group * columns + second, unit].astype(jnp.float32)
            for window in range(windows):
                lanes = slice(window * BLK, (window + 1) * BLK)
                a_real, a_imag = a[:UNIT, lanes], a[UNIT:, lanes]
                b_real, b_imag = b[:UNIT, lanes], b[UNIT:, lanes]
                real += a_real * b_real + a_imag * b_imag
                imag += a_real * b_imag - a_imag * b_real
        return jnp.concatenate([real, imag], axis=0) * scale

    def cross_entries(sub, column, out_ref):
        for entry in range(entries):
            first = lists_smem[column, 0, 2 * entry]
            second = lists_smem[column, 0, 2 * entry + 1]
            out_ref[entry] = cross(sub, first, second).astype(jnp.bfloat16)

    def slot_lane(slot, place):
        return 2 * entries + 4 * slot + place

    def cross_slots(sub, column):
        for group in range(groups):
            for rank in range(CAP):
                slot = group * CAP + rank
                first = lists_smem[column, 0, slot_lane(slot, 0)]
                second = lists_smem[column, 0, slot_lane(slot, 1)]
                used = lists_smem[column, 0, slot_lane(slot, 2)].astype(jnp.float32)
                block = cross(sub, first, second) * used
                slot_buf[group, column, rank] = block.astype(jnp.bfloat16)

    def swap_copy(sub, step):
        return pltpu.make_async_remote_copy(
            src_ref=swap_bufs[sub].at[step - 1],
            dst_ref=entry_bufs[sub][step],
            send_sem=hsend_sem.at[sub, step],
            recv_sem=hrecv_sem.at[sub, step],
            device_id=(my_group, lax.rem(mine + step, columns)),
            device_id_type=MESH,
        )

    def forward_copy(sub, other, source):
        return pltpu.make_async_remote_copy(
            src_ref=forward_bufs[sub].at[other - 1, source],
            dst_ref=stack_bufs[sub].at[:, my_group * columns + source],
            send_sem=fsend_sem.at[sub],
            recv_sem=frecv_sem.at[sub, my_group],
            device_id=(group_at(other), mine),
            device_id_type=MESH,
        )

    def slot_copy(group, column):
        return pltpu.make_async_remote_copy(
            src_ref=slot_buf.at[group, column],
            dst_ref=stack_bufs[hops].at[:, me],
            send_sem=ssend_sem.at[0],
            recv_sem=srecv_sem.at[0],
            device_id=(group, column),
            device_id_type=MESH,
        )

    slot_own = pltpu.make_async_copy(
        slot_buf.at[my_group, mine], stack_bufs[hops].at[:, me], own_sem.at[2]
    )

    def arrived(ref, sem):
        return pltpu.make_async_remote_copy(
            src_ref=ref,
            dst_ref=ref,
            send_sem=sem,
            recv_sem=sem,
            device_id=(lax.rem(my_group + 1, groups), mine),
            device_id_type=MESH,
        )

    def forward(sub, step):
        source = lax.rem(mine - step + columns, columns)
        if step > 0:
            swap_copy(sub, step).wait_recv()
        for other in range(groups):
            for rank in range(CAP):
                slot = group_at(other) * CAP + rank
                used = lists_smem[mine, 0, slot_lane(slot, 2)].astype(jnp.float32)
                entry = lists_smem[mine, 0, slot_lane(slot, 3)]
                block = (entry_bufs[sub][step][entry].astype(jnp.float32) * used).astype(jnp.bfloat16)
                if other == 0:
                    stack_bufs[sub][rank, my_group * columns + source] = block
                else:
                    forward_bufs[sub][other - 1, source, rank] = block
            if other > 0:
                forward_copy(sub, other, source).start()

    def cross_sub(sub):
        if sub % wave_subs == 0:
            wave = sub // wave_subs
            white_own(wave).wait()
            arrived(rows_bufs[wave].at[pl.ds(0, devices - 1)], wrecv_sem.at[wave]).wait_recv()
        if sub < hops:

            def entries_step(step):
                cross_entries(sub, lax.rem(mine + step, columns), swap_bufs[sub].at[step - 1])
                for place in range(1, columns):

                    @pl.when(step == place)
                    def _():
                        swap_copy(sub, place).start()

            loop(1, columns, entries_step)
            cross_entries(sub, mine, entry_bufs[sub][0])
        else:

            def slots_step(step):
                column = lax.rem(mine + step, columns)
                cross_slots(sub, column)
                for other in range(groups):
                    group = group_at(other)
                    if other > 0:
                        slot_copy(group, column).start()
                    else:

                        @pl.when(step < columns)
                        def _():
                            slot_copy(group, column).start()

                        @pl.when(step == columns)
                        def _():
                            slot_own.start()

            loop(1, columns + 1, slots_step)

    def wait_stack(sub):
        def wait(other):
            group = group_at(other)
            part = stack_bufs[sub].at[:, pl.ds(group * columns, columns)]
            arrived(part, frecv_sem.at[sub, group]).wait_recv()

        loop(1, groups, wait)

    for sub in range(subs):
        cross_sub(sub)
        if sub == 0 and last > 0:
            for copy in inverse_copies:
                copy.start()
        for step in range(columns if 0 < sub else 0):
            forward(sub - 1, step)
    for sub in range(last):
        wait_stack(sub)
    if last > 0:
        for copy in inverse_copies:
            copy.wait()
        transposed(stack_bufs[:last], left_buf)

        def odd_lags(tile):
            at = pl.ds(pl.multiple_of(tile * LAGS, LAGS), LAGS)
            odd_ref[:, at] = jnp.dot(
                left_buf[...], inverse_buf[:, at], preferred_element_type=jnp.float32
            )

        loop(0, NFFT // 2 // LAGS, odd_lags)
    for wave in range(waves):
        arrived(rows_bufs[wave].at[pl.ds(0, devices - 1)], wsend_sem.at[wave]).wait_send()
    for sub in range(hops):
        for step in range(1, columns):
            swap_copy(sub, step).wait_send()
        arrived(forward_bufs[sub], fsend_sem.at[sub]).wait_send()
    for sub in range(last, hops):
        wait_stack(sub)
    others = stack_bufs[hops].at[:, pl.ds(0, devices - 1)]
    arrived(others, ssend_sem.at[0]).wait_send()
    slot_own.wait()
    arrived(others, srecv_sem.at[0]).wait_recv()


def lags_kernel(*refs):
    stack_refs = refs[:-6]
    odd_ref, inverse_ref, out_hbm, left_buf, out_buf, out_sem = refs[-6:]
    transposed(stack_refs, left_buf)
    count = NFFT // 2 // LAGS

    def copies(tile):
        for side in range(2):
            at = pl.ds(side * (NFFT // 2) + tile * LAGS, LAGS)
            yield pltpu.make_async_copy(
                out_buf.at[:, at], out_hbm.at[:, at], out_sem.at[side, tile]
            )

    for tile in range(count):
        at = slice(tile * LAGS, (tile + 1) * LAGS)
        upper = slice(NFFT // 2 + tile * LAGS, NFFT // 2 + (tile + 1) * LAGS)
        even = jnp.dot(left_buf[...], inverse_ref[:, at], preferred_element_type=jnp.float32)
        odd = odd_ref[:, at]
        out_buf[:, at] = even - odd
        out_buf[:, upper] = even + odd
        for copy in copies(tile):
            copy.start()
    for tile in range(count):
        for copy in copies(tile):
            copy.wait()


def local(strain, valid_mask, pair_list, owner_group):
    windows, channels = valid_mask.shape
    groups = lax.axis_size("grp")
    columns = lax.axis_size("ch")
    devices = groups * columns
    entries = owner_group.shape[1]
    phases = phases_of(devices)
    rows = 2 * NB // devices // phases
    lanes = windows * channels
    tiles = NB // (columns * UNIT * phases)
    tile_rows = 2 * NB // tiles
    scale = 1.0 / math.sqrt(NB * windows * groups)

    vmem = pl.BlockSpec(memory_space=pltpu.VMEM)
    anywhere = pl.BlockSpec(memory_space=pltpu.HBM)
    dma = pltpu.SemaphoreType.DMA
    bf16 = jnp.bfloat16
    depth = devices * rows
    per_group = tiles // groups
    subs = phases * per_group
    hops = subs - 1
    waves = min(WAVES, phases)
    last = subs - per_group if phases > 1 else 0
    unit_rows = 2 * UNIT
    stack_shape = (CAP, devices, unit_rows, BLK)
    outs = [jax.ShapeDtypeStruct(stack_shape, bf16) for _ in range(subs - last)]
    if phases > 1:
        outs.append(jax.ShapeDtypeStruct((CAP * BLK, NFFT // 2), jnp.float32))
        outs.append(jax.ShapeDtypeStruct((NB, NFFT // 2), bf16))
    inverse = inverse_rows(groups, columns)
    first_shape = inverse.shape[1:] if phases > 1 else (16, LANES)
    stacks = pl.pallas_call(
        functools.partial(correlate_kernel, groups, columns, phases, entries, windows, scale),
        out_shape=outs,
        in_specs=[anywhere] * 6,
        out_specs=[vmem] * len(outs),
        scratch_shapes=[
            pltpu.SMEM((1, 2, entries), jnp.int32),
            pltpu.SMEM((1, entries), jnp.int32),
            pltpu.VMEM((windows, channels), jnp.int32),
            pltpu.VMEM((lanes, NFFT), bf16),
            pltpu.VMEM(first_shape, bf16),
            pltpu.VMEM((CAP * BLK, depth), bf16),
            pltpu.VMEM((tiles, tile_rows, NFFT), bf16),
            pltpu.VMEM((groups, waves, columns, subs // waves * unit_rows, lanes), bf16),
            pltpu.VMEM((8, LANES), jnp.int32),
            pltpu.VMEM((columns, 8, LANES), jnp.int32),
            pltpu.SMEM((columns, 8, LANES), jnp.int32),
            pltpu.VMEM((groups, columns, CAP, unit_rows, BLK), bf16),
        ]
        + [
            pltpu.VMEM((devices, subs // waves * unit_rows, lanes), bf16)
            for _ in range(waves)
        ]
        + [pltpu.VMEM((columns - 1, entries, unit_rows, BLK), bf16) for _ in range(hops)]
        + [pltpu.VMEM((groups - 1, columns, CAP, unit_rows, BLK), bf16) for _ in range(hops)]
        + [pltpu.VMEM((entries, unit_rows, BLK), bf16) for _ in range(hops * columns)]
        + [pltpu.VMEM(stack_shape, bf16) for _ in range(last)]
        + [dma((4,)), dma((2,)), dma((tiles,)), dma((3,)), dma((columns,)), dma((columns,))]
        + [dma((waves,)), dma((waves,)), dma((waves,))]
        + [dma((max(1, hops), columns)), dma((max(1, hops), columns))]
        + [dma((max(1, hops),)), dma((max(1, hops), groups)), dma((1,)), dma((1,))],
        compiler_params=pltpu.CompilerParams(
            collective_id=0, has_side_effects=True, vmem_limit_bytes=44 * 1024 * 1024
        ),
    )(
        *[
            pltpu.with_memory_space_constraint(operand, pltpu.HBM)
            for operand in (
                pair_list.transpose(0, 2, 1),
                owner_group,
                valid_mask,
                strain.reshape(lanes, NFFT),
                jnp.asarray(forward_rows(groups, columns)).reshape(tiles, tile_rows, NFFT),
                jnp.asarray(inverse if phases > 1 else np.zeros(first_shape, bf16)),
            )
        ]
    )
    if phases > 1:
        stacked = pl.pallas_call(
            lags_kernel,
            out_shape=jax.ShapeDtypeStruct((CAP * BLK, NFFT), jnp.float32),
            in_specs=[vmem] * len(outs),
            out_specs=anywhere,
            scratch_shapes=[
                pltpu.VMEM((CAP * BLK, depth), bf16),
                pltpu.VMEM((CAP * BLK, NFFT), jnp.float32),
                dma((2, NFFT // 2 // LAGS)),
            ],
            compiler_params=pltpu.CompilerParams(vmem_limit_bytes=44 * 1024 * 1024),
        )(*stacks)
    else:
        stacked = jnp.einsum(
            "skr,kt->srt",
            stacks[0].reshape(CAP, depth, BLK),
            jnp.asarray(inverse[0]),
            preferred_element_type=jnp.float32,
        )
    return stacked.reshape(1, 1, CAP, BLK, NFFT)


def solution(mesh):
    placed = (P("grp", "ch", None), P("grp", "ch"), P("ch", None, None), P("ch", None))
    return jax.shard_map(
        local,
        mesh=mesh,
        in_specs=placed,
        out_specs=P("grp", "ch", None, None, None),
        check_vma=False,
    )
```
